128 devices in a mesh: grp: 4 (over y), row: 32 (over x, z, core).
Axes of the slice: x: 4, y: 4, z: 4, core: 2. Of those that a mesh axis runs over, the one named last changes fastest.
Arguments:
- b_tensor: bfloat16 [9984, 8, 768], P(None, 'grp', 'row'), may hold values from -0.21875 to 0.21875
- aux_counts: int32 [4], replicated, may hold values from 1 to 2, as said below
Outputs:
- exchange_matrix: float32 [9984, 9984], P('row', 'grp')
The draws below stay inside these ranges and needn't reach their ends.
Inputs may be any that keep to these rules, and one draw needn't show every extreme that they name: `aux_counts`: some group has all 2 slots live.
All inputs are finite; a program needn't handle non-finite values.
Results may differ from the reference program's by a relative error of at most 0.0003.
Values may be sent and summed in bfloat16 or wider, within the bound.
No kernel may reach another device: no remote copies, remote signals or barrier semaphores. Data moves between devices by JAX's collectives and lax.ppermute only.
A program may use at most 128 MiB of HBM per device.

```python
import jax
import jax.numpy as jnp
from jax import lax

NBF = 9984
NOCC = 768
APG = 2
SLOTS = 8
N_GRP = 4


def draw_aux_counts(key, part):
    counts = jax.random.randint(key, (N_GRP,), 1, APG + 1)
    chosen = jax.random.randint(jax.random.fold_in(key, 7), (), 0, N_GRP)
    return counts.at[chosen].set(APG).astype(jnp.int32)


def steps_of(own_key, shape, cuts, least, largest):
    def one(axis_at, shards_of):
        steps = jax.random.uniform(jax.random.fold_in(jax.random.fold_in(own_key, 6), axis_at), (shards_of,), jnp.float32, least / len(cuts), largest / len(cuts))
        return jnp.repeat(jnp.exp(steps), shape[axis_at] // shards_of).reshape((-1,) + (1,) * (len(shape) - axis_at - 1))

    gain = one(*cuts[0])
    for cut in cuts[1:]:
        gain = gain * one(*cut)
    return gain


def normal_values(stream_key, shape, width, bound, split=(), kind=jnp.bfloat16):
    values = width * jax.random.normal(stream_key, shape, jnp.float32)
    if split:
        values = values * steps_of(stream_key, shape, split, -0.22, 0.18)
    return jnp.clip(values, -bound, bound).astype(kind)


def setup_inputs(seed: int = 0) -> dict:
    seeds = jax.random.split(jax.random.key(seed), 3)
    return {
        "b_tensor": normal_values(seeds[0], (NBF, SLOTS, NOCC), NOCC ** -0.5, 0.21875, ((1, 4), (2, 32))),
        "aux_counts": draw_aux_counts(jax.random.fold_in(seeds[2], 71), 0),
    }


def reference(b_tensor, aux_counts):
    slot_index = jnp.arange(SLOTS)
    group_of = slot_index // APG
    live_mask = (slot_index % APG) < aux_counts[group_of]
    masked = b_tensor * live_mask.astype(jnp.bfloat16)[None, :, None]
    stacked = masked.reshape(NBF, SLOTS * NOCC).astype(jnp.float32)
    return jnp.dot(stacked, stacked.T, precision=lax.Precision.HIGHEST, preferred_element_type=jnp.float32)
```

```python
import jax
import jax.numpy as jnp
from jax import lax
from jax.sharding import Mesh, PartitionSpec as P


SIDE = 4
CORES = 2
WIDE = 1280
HALF = WIDE // 2


def shift(block, axis, step):
    return lax.ppermute(block, axis, [(i, (i + step) % SIDE) for i in range(SIDE)])


def swap_cores(block):
    return lax.ppermute(block, "core", [(0, 1), (1, 0)])


def rolled(blocks, start):
    n = blocks.shape[0]
    return jnp.stack([lax.dynamic_index_in_dim(blocks, (start + i) % n, 0, keepdims=False) for i in range(n)])


def gathered(own, first, second):
    rows = own.shape[0]
    mid = rows // 2
    near = {0: own, -1: shift(own, first, 1), 1: shift(own, first, -1)}
    near[2] = shift(near[-1], first, 1)
    parts = {}
    for u, block in near.items():
        left, right = shift(block, second, 1), shift(block, second, -1)
        parts[u, 0] = [(0, rows, block)]
        parts[u, -1] = [(0, rows, left)]
        parts[u, 1] = [(0, rows, right)]
        if u == 0:
            parts[u, 2] = [(0, rows, shift(left, second, 1))]
        elif u == -1:
            parts[u, 2] = [
                (0, mid, shift(left[:mid], second, 1)),
                (mid, rows, shift(right[mid:], second, -1)),
            ]
        else:
            parts[u, 2] = [(0, rows, shift(right, second, -1))]
    return parts


def shards(b_tensor, aux_counts):
    basis = b_tensor.shape[0]
    slots = b_tensor.shape[1]
    x, y, z, core = (lax.axis_index(name) for name in ("x", "y", "z", "core"))
    live_count = lax.dynamic_index_in_dim(aux_counts, y, 0, keepdims=False)
    live = (jnp.arange(slots) < live_count).astype(jnp.bfloat16)
    terms = (b_tensor * live[None, :, None]).transpose(1, 2, 0).reshape(-1, basis)
    depth = terms.shape[0]

    block_columns = basis // SIDE
    padded = jnp.pad(terms, ((0, 0), (0, CORES * WIDE - block_columns)))
    windows = jnp.stack(
        [
            padded[:, p * block_columns + q * WIDE : p * block_columns + (q + 1) * WIDE]
            for p in range(SIDE)
            for q in range(CORES)
        ]
    )
    columns = lax.all_to_all(windows, ("y", "core"), 0, 0, tiled=True)

    chip_rows = basis // (SIDE * SIDE)
    rows = lax.all_to_all(
        terms.reshape(depth, SIDE * SIDE, chip_rows).transpose(1, 0, 2), ("x", "z"), 0, 0, tiled=True
    )
    rows = rows.reshape(SIDE, SIDE, depth, chip_rows)
    rows = rolled(rolled(rows, x).transpose(1, 0, 2, 3), z)

    columns = columns.reshape(SIDE, CORES, depth, WIDE)
    columns = rolled(rolled(columns, y).transpose(1, 0, 2, 3), core)
    columns = columns.reshape(CORES * SIDE * depth, WIDE)

    mid = SIDE // 2
    left, right = shift(rows, "y", 1), shift(rows, "y", -1)
    far = jnp.concatenate([shift(left[:mid], "y", 1), shift(right[mid:], "y", -1)])
    mine = jnp.stack([rows, right, far, left])
    both = jnp.stack([mine, swap_cores(mine)])

    a = gathered(columns[:, :HALF], "x", "z")
    b = gathered(columns[:, HALF:], "z", "x")

    def tile(parts, along_x_first):
        total = jnp.zeros((chip_rows, HALF), jnp.float32)
        for (u, v), ranges in parts.items():
            dx, dz = (u, v) if along_x_first else (v, u)
            weights = both[:, :, dz % SIDE, dx % SIDE].reshape(CORES * SIDE * depth, chip_rows)
            for low, high, block in ranges:
                total = total + lax.dot_general(
                    weights[low:high],
                    block,
                    (((0,), (0,)), ((), ())),
                    preferred_element_type=jnp.float32,
                )
        return total

    out = jnp.concatenate([tile(a, True), tile(b, False)], axis=1)
    out = out.reshape(CORES, chip_rows // CORES, WIDE)
    kept = lax.dynamic_index_in_dim(out, core, 0, keepdims=False)
    got = swap_cores(lax.dynamic_index_in_dim(out, 1 - core, 0, keepdims=False))
    first = jnp.where(core == 0, kept, got)
    last = jnp.where(core == 0, got, kept)
    return jnp.concatenate([first, last[:, : block_columns - WIDE]], axis=1)


def solution(mesh):
    fine = Mesh(mesh.devices.reshape(SIDE, SIDE, SIDE, CORES), ("y", "x", "z", "core"))
    return jax.shard_map(
        shards,
        mesh=fine,
        in_specs=(P(None, "y", ("x", "z", "core")), P()),
        out_specs=P(("x", "z", "core"), "y"),
        check_vma=False,
    )
```

```python
import jax
import jax.numpy as jnp
from jax import lax
from jax.experimental import pallas as pl
from jax.experimental.pallas import tpu as pltpu
from jax.sharding import Mesh, PartitionSpec as P


SIDE = 4
CORES = 2
WIDE = 1280
HALF = WIDE // 2
VMEM = pl.BlockSpec(memory_space=pltpu.VMEM)
SMEM = pl.BlockSpec(memory_space=pltpu.SMEM)


def shift(block, axis, step):
    return lax.ppermute(block, axis, [(i, (i + step) % SIDE) for i in range(SIDE)])


def swap_cores(block):
    return lax.ppermute(block, "core", [(0, 1), (1, 0)])


def rolled(blocks, start):
    n = blocks.shape[0]
    return jnp.stack([lax.dynamic_index_in_dim(blocks, (start + i) % n, 0, keepdims=False) for i in range(n)])


def pack_kernel(place_ref, terms_ref, *refs):
    window_refs, rows_ref, windows = refs[: SIDE * CORES], refs[-2], refs[-1]
    slots, orbitals, basis = terms_ref.shape
    columns = basis // SIDE
    chip_rows = rows_ref.shape[2]
    count, y, core = place_ref[0], place_ref[1], place_ref[2]
    for s in range(slots):
        live = s < count
        at = pl.ds(s * orbitals, orbitals)
        for p in range(SIDE):
            for q in range(CORES):
                start = p * columns + q * WIDE
                width = min(WIDE, basis - start)
                block = terms_ref[s, :, start : start + width]
                windows[p * CORES + q, at, :width] = jnp.where(live, block, jnp.zeros_like(block))
                if width < WIDE:
                    windows[p * CORES + q, at, width:] = jnp.zeros((orbitals, WIDE - width), block.dtype)
        for i in range(SIDE * SIDE):
            block = terms_ref[s, :, i * chip_rows : (i + 1) * chip_rows]
            rows_ref[i, at, :] = jnp.where(live, block, jnp.zeros_like(block))
    for dcore in range(CORES):
        for dy in range(SIDE):
            to = lax.rem(y + dy, SIDE) * CORES + lax.rem(core + dcore, CORES)
            window_refs[dcore * SIDE + dy][...] = windows[to]


def pack(place, terms):
    slots, orbitals, basis = terms.shape
    depth = slots * orbitals
    window = jax.ShapeDtypeStruct((depth, WIDE), terms.dtype)
    chip_rows = jax.ShapeDtypeStruct((SIDE * SIDE, depth, basis // (SIDE * SIDE)), terms.dtype)
    *windows, rows = pl.pallas_call(
        pack_kernel,
        out_shape=(window,) * (SIDE * CORES) + (chip_rows,),
        in_specs=[SMEM, VMEM],
        out_specs=(VMEM,) * (SIDE * CORES + 1),
        scratch_shapes=[pltpu.VMEM((SIDE * CORES, depth, WIDE), terms.dtype)],
        compiler_params=pltpu.CompilerParams(vmem_limit_bytes=10 << 20),
        name="pack",
    )(place, terms)
    return windows, rows


def exchanged(windows):
    from_offset = {}
    for dcore in range(CORES):
        for dy in (2, 1, 3, 0):
            block = windows[dcore * SIDE + dy]
            if dy or dcore:
                route = [
                    (y * CORES + core, (y + dy) % SIDE * CORES + (core + dcore) % CORES)
                    for y in range(SIDE)
                    for core in range(CORES)
                ]
                block = lax.ppermute(block, ("y", "core"), route)
            from_offset[dcore, -dy % SIDE] = block
    return jnp.concatenate([from_offset[dcore, dy] for dcore in range(CORES) for dy in range(SIDE)])


def assemble_kernel(core_ref, a_ref, b_ref, a_got_ref, b_got_ref, out_ref):
    rest = out_ref.shape[1] - WIDE
    for core in range(CORES):

        @pl.when(core_ref[0] == core)
        def _():
            mine, other = (0, WIDE) if core == 0 else (WIDE, 0)
            for at, a, b in ((mine, a_ref[core], b_ref[core]), (other, a_got_ref[...], b_got_ref[...])):
                out_ref[:, at : at + HALF] = a
                if at:
                    out_ref[:, at + HALF :] = b[:, : rest - HALF]
                else:
                    out_ref[:, at + HALF : at + WIDE] = b


def assemble(core, a, b, a_got, b_got, columns):
    return pl.pallas_call(
        assemble_kernel,
        out_shape=jax.ShapeDtypeStruct((a.shape[1], columns), a.dtype),
        in_specs=[SMEM, VMEM, VMEM, VMEM, VMEM],
        out_specs=VMEM,
        compiler_params=pltpu.CompilerParams(vmem_limit_bytes=20 << 20),
        name="assemble",
    )(core.reshape(1), a, b, a_got, b_got)


def gathered(own, first, second):
    rows = own.shape[0]
    mid = rows // 2
    near = {0: own, -1: shift(own, first, 1), 1: shift(own, first, -1)}
    near[2] = shift(near[-1], first, 1)
    sides = {u: (shift(block, second, 1), shift(block, second, -1)) for u, block in near.items()}
    parts = [(u, 0, 0, rows, block) for u, block in near.items()]
    for u, (left, right) in sides.items():
        parts += [(u, -1, 0, rows, left), (u, 1, 0, rows, right)]
    for u, (left, right) in sides.items():
        if u == 0:
            parts.append((u, 2, 0, rows, shift(left, second, 1)))
        elif u == -1:
            parts.append((u, 2, 0, mid, shift(left[:mid], second, 1)))
            parts.append((u, 2, mid, rows, shift(right[mid:], second, -1)))
        else:
            parts.append((u, 2, 0, rows, shift(right, second, -1)))
    return parts


def body(b_tensor, aux_counts):
    basis = b_tensor.shape[0]
    x, y, z, core = (lax.axis_index(name) for name in ("x", "y", "z", "core"))
    count = lax.dynamic_index_in_dim(aux_counts, y, 0, keepdims=False)
    windows, rows = pack(jnp.stack([count, y, core]), b_tensor.transpose(1, 2, 0))
    depth, chip_rows = rows.shape[1:]

    columns = exchanged(windows)
    rows = lax.all_to_all(rows, ("x", "z"), 0, 0, tiled=True)
    rows = rows.reshape(SIDE, SIDE, depth, chip_rows)
    rows = rolled(rolled(rows, x).transpose(1, 0, 2, 3), z)

    a = gathered(columns[:, :HALF], "x", "z")
    b = gathered(columns[:, HALF:], "z", "x")

    mid = SIDE // 2
    left, right = shift(rows, "y", 1), shift(rows, "y", -1)
    far = (shift(left[:mid], "y", 1), shift(right[mid:], "y", -1))
    mine = [[rows], [right], list(far), [left]]
    other = [[swap_cores(block) for block in blocks] for blocks in mine]
    held = mine + other

    def weights(dx, dz):
        return jnp.concatenate(
            [blocks[0][dz, dx] if len(blocks) == 1 else blocks[dz // mid][dz % mid, dx] for blocks in held]
        )

    total = {"a": jnp.zeros((chip_rows, HALF), jnp.float32), "b": jnp.zeros((chip_rows, HALF), jnp.float32)}
    for part_a, part_b in zip(a, b):
        for name, (u, v, low, high, block) in (("a", part_a), ("b", part_b)):
            dx, dz = (u, v) if name == "a" else (v, u)
            product = lax.dot_general(
                weights(dx % SIDE, dz % SIDE)[low:high],
                block,
                (((0,), (0,)), ((), ())),
                preferred_element_type=jnp.float32,
            )
            total[name] = lax.optimization_barrier(total[name] + product)

    tiles, got = [], []
    for name in ("a", "b"):
        tile = total[name].reshape(CORES, chip_rows // CORES, HALF)
        tiles.append(tile)
        got.append(swap_cores(lax.dynamic_index_in_dim(tile, 1 - core, 0, keepdims=False)))
    return assemble(core, *tiles, *got, basis // SIDE)


def solution(mesh):
    fine = Mesh(mesh.devices.reshape(SIDE, SIDE, SIDE, CORES), ("y", "x", "z", "core"))
    return jax.shard_map(
        body,
        mesh=fine,
        in_specs=(P(None, "y", ("x", "z", "core")), P()),
        out_specs=P(("x", "z", "core"), "y"),
        check_vma=False,
    )
```

```python
import jax
import jax.numpy as jnp
from jax import lax
from jax.experimental import pallas as pl
from jax.experimental.pallas import tpu as pltpu
from jax.sharding import Mesh, PartitionSpec as P


SIDE = 4
CORES = 2
PLANE = SIDE * SIDE
SOURCES = CORES * SIDE
WIDE = 1280
VMEM = pl.BlockSpec(memory_space=pltpu.VMEM)
SMEM = pl.BlockSpec(memory_space=pltpu.SMEM)


def along_y(block, step):
    return lax.ppermute(block, "y", [(i, (i + step) % SIDE) for i in range(SIDE)])


def swap_cores(block):
    return lax.ppermute(block, "core", [(0, 1), (1, 0)])


def along_plane(block, order, step):
    route = []
    for x in range(SIDE):
        for z in range(SIDE):
            for core in range(CORES):
                to = ((x + step) % SIDE, z) if core == order else (x, (z + step) % SIDE)
                route.append(((x * SIDE + z) * CORES + core, (to[0] * SIDE + to[1]) * CORES + core))
    return lax.ppermute(block, ("x", "z", "core"), route)


def join(blocks):
    def kernel(*refs):
        at = 0
        for ref in refs[:-1]:
            refs[-1][at : at + ref.shape[0]] = ref[...]
            at += ref.shape[0]

    total = sum(block.shape[0] for block in blocks)
    joined = jax.ShapeDtypeStruct((total, *blocks[0].shape[1:]), blocks[0].dtype)
    size = joined.size * joined.dtype.itemsize
    return pl.pallas_call(
        kernel,
        out_shape=joined,
        in_specs=[VMEM] * len(blocks),
        out_specs=VMEM,
        compiler_params=pltpu.CompilerParams(vmem_limit_bytes=4 * size),
        cost_estimate=pl.CostEstimate(flops=0, bytes_accessed=2 * size, transcendentals=0),
        name="join",
    )(*blocks)


def pack_kernel(count_ref, terms_ref, *refs):
    window_refs, rows_ref, windows = refs[:SOURCES], refs[-2], refs[-1]
    slots, orbitals, basis = terms_ref.shape
    columns = basis // SIDE
    chip_rows = rows_ref.shape[2]
    y, core = lax.axis_index("y"), lax.axis_index("core")
    for s in range(slots):
        live = s < count_ref[y]
        at = pl.ds(s * orbitals, orbitals)
        for p in range(SIDE):
            for q in range(CORES):
                start = p * columns + q * WIDE
                width = min(WIDE, basis - start)
                block = terms_ref[s, :, start : start + width]
                windows[p * CORES + q, at, :width] = jnp.where(live, block, jnp.zeros_like(block))
                if width < WIDE:
                    windows[p * CORES + q, at, width:] = jnp.zeros((orbitals, WIDE - width), block.dtype)
        for i in range(PLANE):
            block = terms_ref[s, :, i * chip_rows : (i + 1) * chip_rows]
            rows_ref[i, at, :] = jnp.where(live, block, jnp.zeros_like(block))
    for dcore in range(CORES):
        for dy in range(SIDE):
            to = lax.rem(y + dy, SIDE) * CORES + lax.rem(core + dcore, CORES)
            window_refs[dcore * SIDE + dy][...] = windows[to]


def pack(counts, terms):
    slots, orbitals, basis = terms.shape
    depth = slots * orbitals
    window = jax.ShapeDtypeStruct((depth, WIDE), terms.dtype)
    chip_rows = jax.ShapeDtypeStruct((PLANE, depth, basis // PLANE), terms.dtype)
    *windows, rows = pl.pallas_call(
        pack_kernel,
        out_shape=(window,) * SOURCES + (chip_rows,),
        in_specs=[SMEM, VMEM],
        out_specs=(VMEM,) * (SOURCES + 1),
        scratch_shapes=[pltpu.VMEM((SOURCES, depth, WIDE), terms.dtype)],
        compiler_params=pltpu.CompilerParams(vmem_limit_bytes=10 << 20),
        name="pack",
    )(counts, terms)
    return windows, rows


def exchanged(windows):
    from_offset = {}
    for dcore in range(CORES):
        for dy in (2, 1, 3, 0):
            block = windows[dcore * SIDE + dy]
            if dy or dcore:
                route = [
                    (y * CORES + core, (y + dy) % SIDE * CORES + (core + dcore) % CORES)
                    for y in range(SIDE)
                    for core in range(CORES)
                ]
                block = lax.ppermute(block, ("y", "core"), route)
            from_offset[dcore, -dy % SIDE] = block
    return join([from_offset[dcore, dy] for dcore in range(CORES) for dy in range(SIDE)])


def gathered(own):
    depth = own.shape[0]
    cut = depth // 2
    before, after = along_plane(own, 0, 1), along_plane(own, 0, -1)
    near = join([before, after])
    own_sides = along_plane(own, 1, 1), along_plane(own, 1, -1)
    near_sides = along_plane(near, 1, 1), along_plane(near, 1, -1)
    far = along_plane(before, 0, 1)
    far_sides = along_plane(far, 1, 1), along_plane(far, 1, -1)
    own_opposite = along_plane(own_sides[0], 1, 1)
    near_opposite = along_plane(near_sides[0][:cut], 1, 1), along_plane(near_sides[1][cut:], 1, -1)
    far_opposite = along_plane(far_sides[1], 1, -1)

    def at(v, *us):
        return tuple((u, v) for u in us)

    parts = [(at(0, 0), 0, own), (at(0, -1, 1), 0, near), (at(0, 2), 0, far)]
    parts += [(at(v, 0), 0, block) for v, block in zip((-1, 1), own_sides)]
    parts += [(at(v, -1, 1), 0, block) for v, block in zip((-1, 1), near_sides)]
    parts += [(at(2, 0), 0, own_opposite)]
    parts += [(at(v, 2), 0, block) for v, block in zip((-1, 1), far_sides)]
    parts += [(at(2, -1, 1), 0, near_opposite[0]), (at(2, -1, 1), SOURCES // 2, near_opposite[1])]
    parts += [(at(2, 2), 0, far_opposite)]
    return parts


def arrange_kernel(layout, rows_ref, rest_ref, other_rows_ref, other_rest_ref, *out_refs):
    depth = rows_ref.shape[1]
    x, z, core = (lax.axis_index(name) for name in ("x", "z", "core"))
    for blocks, out_ref in zip(layout, out_refs):
        for i, (u, v, source) in enumerate(blocks):
            dx, dz = jnp.where(core == 0, u, v), jnp.where(core == 0, v, u)
            chip = lax.rem(x + dx + SIDE, SIDE) * SIDE + lax.rem(z + dz + SIDE, SIDE)
            dcore, dy = divmod(source, SIDE)
            if dy == 0:
                block = (rows_ref, other_rows_ref)[dcore][chip]
            else:
                block = (rest_ref, other_rest_ref)[dcore][(dy - 1) * PLANE + chip]
            out_ref[i * depth : (i + 1) * depth, :] = block


def arrange(layout, rows, rest, other_rows, other_rest):
    depth, chip_rows = rows.shape[1:]
    return pl.pallas_call(
        lambda *refs: arrange_kernel(layout, *refs),
        out_shape=tuple(jax.ShapeDtypeStruct((len(blocks) * depth, chip_rows), rows.dtype) for blocks in layout),
        in_specs=[VMEM] * 4,
        out_specs=(VMEM,) * len(layout),
        compiler_params=pltpu.CompilerParams(vmem_limit_bytes=20 << 20),
        name="arrange",
    )(rows, rest, other_rows, other_rest)


def assemble_kernel(tile_ref, got_ref, out_ref):
    rest = out_ref.shape[1] - WIDE
    for core in range(CORES):

        @pl.when(lax.axis_index("core") == core)
        def _():
            first, last = (tile_ref.at[core], got_ref) if core == 0 else (got_ref, tile_ref.at[core])
            out_ref[:, :WIDE] = first[...]
            out_ref[:, WIDE:] = last[:, :rest]


def assemble(tile, got, columns):
    return pl.pallas_call(
        assemble_kernel,
        out_shape=jax.ShapeDtypeStruct((got.shape[0], columns), got.dtype),
        in_specs=[VMEM, VMEM],
        out_specs=VMEM,
        compiler_params=pltpu.CompilerParams(vmem_limit_bytes=20 << 20),
        name="assemble",
    )(tile, got)


def body(b_tensor, aux_counts):
    basis = b_tensor.shape[0]
    core = lax.axis_index("core")
    windows, rows = pack(aux_counts, b_tensor.transpose(1, 2, 0))
    chip_rows = rows.shape[2]

    columns = exchanged(windows)
    rows = lax.all_to_all(rows, ("x", "z"), 0, 0, tiled=True)
    parts = gathered(columns)

    left, right = along_y(rows, 1), along_y(rows, -1)
    half = PLANE // 2
    far = along_y(left[:half], 1), along_y(right[half:], -1)
    rest = join([right, *far, left])
    other_rows = swap_cores(rows)
    other_rest = swap_cores(rest)

    layout = []
    for offsets, skipped, block in parts:
        blocks = [(u, v, source) for u, v in offsets for source in range(SOURCES)]
        layout.append(blocks[skipped : skipped + block.shape[0] // rows.shape[1]])
    weights = arrange(layout, rows, rest, other_rows, other_rest)

    tile = None
    for (_, _, block), weight in zip(parts, weights):
        product = lax.dot_general(weight, block, (((0,), (0,)), ((), ())), preferred_element_type=jnp.float32)
        tile = lax.optimization_barrier(product if tile is None else tile + product)

    tile = tile.reshape(CORES, chip_rows // CORES, WIDE)
    got = swap_cores(lax.dynamic_index_in_dim(tile, 1 - core, 0, keepdims=False))
    return assemble(tile, got, basis // SIDE)


def solution(mesh):
    fine = Mesh(mesh.devices.reshape(SIDE, SIDE, SIDE, CORES), ("y", "x", "z", "core"))
    return jax.shard_map(
        body,
        mesh=fine,
        in_specs=(P(None, "y", ("x", "z", "core")), P()),
        out_specs=P(("x", "z", "core"), "y"),
        check_vma=False,
    )
```

```python
import jax
import jax.numpy as jnp
from jax import lax
from jax.experimental import pallas as pl
from jax.experimental.pallas import tpu as pltpu
from jax.sharding import Mesh, PartitionSpec as P


SIDE = 4
CORES = 2
PLANE = SIDE * SIDE
SOURCES = CORES * SIDE
WIDE = 1280
VMEM = pl.BlockSpec(memory_space=pltpu.VMEM)
SMEM = pl.BlockSpec(memory_space=pltpu.SMEM)


def along_y(block, step):
    return lax.ppermute(block, "y", [(i, (i + step) % SIDE) for i in range(SIDE)])


def swap_cores(block):
    return lax.ppermute(block, "core", [(0, 1), (1, 0)])


def along_plane(block, order, step):
    route = []
    for x in range(SIDE):
        for z in range(SIDE):
            for core in range(CORES):
                to = ((x + step) % SIDE, z) if core == order else (x, (z + step) % SIDE)
                route.append(((x * SIDE + z) * CORES + core, (to[0] * SIDE + to[1]) * CORES + core))
    return lax.ppermute(block, ("x", "z", "core"), route)


def join(blocks):
    def kernel(*refs):
        at = 0
        for ref in refs[:-1]:
            refs[-1][at : at + ref.shape[0]] = ref[...]
            at += ref.shape[0]

    total = sum(block.shape[0] for block in blocks)
    joined = jax.ShapeDtypeStruct((total, *blocks[0].shape[1:]), blocks[0].dtype)
    size = joined.size * joined.dtype.itemsize
    return pl.pallas_call(
        kernel,
        out_shape=joined,
        in_specs=[VMEM] * len(blocks),
        out_specs=VMEM,
        compiler_params=pltpu.CompilerParams(vmem_limit_bytes=2 * size + (1 << 18)),
        cost_estimate=pl.CostEstimate(flops=0, bytes_accessed=2 * size, transcendentals=0),
        name="join",
    )(*blocks)


def pack_kernel(count_ref, terms_ref, *refs):
    window_refs, rows_ref, windows = refs[:SOURCES], refs[-2], refs[-1]
    slots, orbitals, basis = terms_ref.shape
    columns = basis // SIDE
    chip_rows = rows_ref.shape[2]
    y, core = lax.axis_index("y"), lax.axis_index("core")
    for s in range(slots):
        live = s < count_ref[y]
        at = pl.ds(s * orbitals, orbitals)
        for p in range(SIDE):
            for q in range(CORES):
                start = p * columns + q * WIDE
                width = min(WIDE, basis - start)
                block = terms_ref[s, :, start : start + width]
                windows[p * CORES + q, at, :width] = jnp.where(live, block, jnp.zeros_like(block))
                if width < WIDE:
                    windows[p * CORES + q, at, width:] = jnp.zeros((orbitals, WIDE - width), block.dtype)
        for i in range(PLANE):
            block = terms_ref[s, :, i * chip_rows : (i + 1) * chip_rows]
            rows_ref[i, at, :] = jnp.where(live, block, jnp.zeros_like(block))
    for dcore in range(CORES):
        for dy in range(SIDE):
            to = lax.rem(y + dy, SIDE) * CORES + lax.rem(core + dcore, CORES)
            window_refs[dcore * SIDE + dy][...] = windows[to]


def pack(counts, terms):
    slots, orbitals, basis = terms.shape
    depth = slots * orbitals
    window = jax.ShapeDtypeStruct((depth, WIDE), terms.dtype)
    chip_rows = jax.ShapeDtypeStruct((PLANE, depth, basis // PLANE), terms.dtype)
    *windows, rows = pl.pallas_call(
        pack_kernel,
        out_shape=(window,) * SOURCES + (chip_rows,),
        in_specs=[SMEM, VMEM],
        out_specs=(VMEM,) * (SOURCES + 1),
        scratch_shapes=[pltpu.VMEM((SOURCES, depth, WIDE), terms.dtype)],
        compiler_params=pltpu.CompilerParams(vmem_limit_bytes=10 << 20),
        name="pack",
    )(counts, terms)
    return windows, rows


def exchanged(windows):
    from_offset = {}
    for dcore in range(CORES):
        for dy in (2, 1, 3, 0):
            block = windows[dcore * SIDE + dy]
            if dy or dcore:
                route = [
                    (y * CORES + core, (y + dy) % SIDE * CORES + (core + dcore) % CORES)
                    for y in range(SIDE)
                    for core in range(CORES)
                ]
                block = lax.ppermute(block, ("y", "core"), route)
            from_offset[dcore, -dy % SIDE] = block
    return join([from_offset[dcore, dy] for dcore in range(CORES) for dy in range(SIDE)])


def gathered(own):
    depth = own.shape[0]
    cut = depth // 2
    before, after = along_plane(own, 0, 1), along_plane(own, 0, -1)
    near = join([before, after])
    own_sides = along_plane(own, 1, 1), along_plane(own, 1, -1)
    near_sides = along_plane(near, 1, 1), along_plane(near, 1, -1)
    far = along_plane(before, 0, 1)
    far_sides = along_plane(far, 1, 1), along_plane(far, 1, -1)
    own_opposite = along_plane(own_sides[0], 1, 1)
    near_opposite = along_plane(near_sides[0][:cut], 1, 1), along_plane(near_sides[1][cut:], 1, -1)
    far_opposite = along_plane(far_sides[1], 1, -1)

    def at(v, *us):
        return tuple((u, v) for u in us)

    parts = [(at(0, 0), 0, own), (at(0, -1, 1), 0, near), (at(0, 2), 0, far)]
    parts += [(at(v, 0), 0, block) for v, block in zip((-1, 1), own_sides)]
    parts += [(at(v, -1, 1), 0, block) for v, block in zip((-1, 1), near_sides)]
    parts += [(at(2, 0), 0, own_opposite)]
    parts += [(at(v, 2), 0, block) for v, block in zip((-1, 1), far_sides)]
    parts += [(at(2, -1, 1), 0, near_opposite[0]), (at(2, -1, 1), SOURCES // 2, near_opposite[1])]
    parts += [(at(2, 2), 0, far_opposite)]
    return parts


def arrange_kernel(layout, rows_ref, rest_ref, other_rows_ref, other_rest_ref, *out_refs):
    depth = rows_ref.shape[1]
    x, z, core = (lax.axis_index(name) for name in ("x", "z", "core"))
    for blocks, out_ref in zip(layout, out_refs):
        for i, (u, v, source) in enumerate(blocks):
            dx, dz = jnp.where(core == 0, u, v), jnp.where(core == 0, v, u)
            chip = lax.rem(x + dx + SIDE, SIDE) * SIDE + lax.rem(z + dz + SIDE, SIDE)
            dcore, dy = divmod(source, SIDE)
            if dy == 0:
                block = (rows_ref, other_rows_ref)[dcore][chip]
            else:
                block = (rest_ref, other_rest_ref)[dcore][(dy - 1) * PLANE + chip]
            out_ref[i * depth : (i + 1) * depth, :] = block


def arrange(layout, rows, rest, other_rows, other_rest):
    depth, chip_rows = rows.shape[1:]
    return pl.pallas_call(
        lambda *refs: arrange_kernel(layout, *refs),
        out_shape=tuple(jax.ShapeDtypeStruct((len(blocks) * depth, chip_rows), rows.dtype) for blocks in layout),
        in_specs=[VMEM] * 4,
        out_specs=(VMEM,) * len(layout),
        compiler_params=pltpu.CompilerParams(vmem_limit_bytes=16 << 20),
        name="arrange",
    )(rows, rest, other_rows, other_rest)


def halve_kernel(tile_ref, kept_ref, sent_ref):
    rows = kept_ref.shape[0]
    for core in range(CORES):

        @pl.when(lax.axis_index("core") == core)
        def _():
            kept_ref[...] = tile_ref[core * rows : (core + 1) * rows, :]
            sent_ref[...] = tile_ref[(1 - core) * rows : (2 - core) * rows, :]


def halve(tile):
    half = jax.ShapeDtypeStruct((tile.shape[0] // CORES, tile.shape[1]), tile.dtype)
    return pl.pallas_call(
        halve_kernel,
        out_shape=(half, half),
        in_specs=[VMEM],
        out_specs=(VMEM, VMEM),
        compiler_params=pltpu.CompilerParams(vmem_limit_bytes=8 << 20),
        name="halve",
    )(tile)


def assemble_kernel(kept_ref, got_ref, out_ref):
    rest = out_ref.shape[1] - WIDE
    for core in range(CORES):

        @pl.when(lax.axis_index("core") == core)
        def _():
            first, last = (kept_ref, got_ref) if core == 0 else (got_ref, kept_ref)
            out_ref[:, :WIDE] = first[...]
            out_ref[:, WIDE:] = last[:, :rest]


def assemble(kept, got, columns):
    return pl.pallas_call(
        assemble_kernel,
        out_shape=jax.ShapeDtypeStruct((got.shape[0], columns), got.dtype),
        in_specs=[VMEM, VMEM],
        out_specs=VMEM,
        compiler_params=pltpu.CompilerParams(vmem_limit_bytes=8 << 20),
        name="assemble",
    )(kept, got)


def body(b_tensor, aux_counts):
    basis = b_tensor.shape[0]
    windows, rows = pack(aux_counts, b_tensor.transpose(1, 2, 0))

    columns = exchanged(windows)
    rows = lax.all_to_all(rows, ("x", "z"), 0, 0, tiled=True)
    parts = gathered(columns)

    left, right = along_y(rows, 1), along_y(rows, -1)
    half = PLANE // 2
    far = along_y(left[:half], 1), along_y(right[half:], -1)
    rest = join([right, *far, left])
    other_rows = swap_cores(rows)
    other_rest = swap_cores(rest)

    layout = []
    for offsets, skipped, block in parts:
        blocks = [(u, v, source) for u, v in offsets for source in range(SOURCES)]
        layout.append(blocks[skipped : skipped + block.shape[0] // rows.shape[1]])
    weights = arrange(layout, rows, rest, other_rows, other_rest)

    tile = None
    for (_, _, block), weight in zip(parts, weights):
        product = lax.dot_general(weight, block, (((0,), (0,)), ((), ())), preferred_element_type=jnp.float32)
        tile = lax.optimization_barrier(product if tile is None else tile + product)

    kept, sent = halve(tile)
    return assemble(kept, swap_cores(sent), basis // SIDE)


def solution(mesh):
    fine = Mesh(mesh.devices.reshape(SIDE, SIDE, SIDE, CORES), ("y", "x", "z", "core"))
    return jax.shard_map(
        body,
        mesh=fine,
        in_specs=(P(None, "y", ("x", "z", "core")), P()),
        out_specs=P(("x", "z", "core"), "y"),
        check_vma=False,
    )
```

```python
import jax
import jax.numpy as jnp
from jax import lax
from jax.experimental import pallas as pl
from jax.experimental.pallas import tpu as pltpu
from jax.sharding import Mesh, PartitionSpec as P


SIDE = 4
CORES = 2
PLANE = SIDE * SIDE
WIDE = 1280
VMEM = pl.BlockSpec(memory_space=pltpu.VMEM)
SMEM = pl.BlockSpec(memory_space=pltpu.SMEM)


def along_y(block, step):
    return lax.ppermute(block, "y", [(i, (i + step) % SIDE) for i in range(SIDE)])


def swap_cores(block):
    return lax.ppermute(block, "core", [(0, 1), (1, 0)])


def along_plane(block, order, step):
    route = []
    for x in range(SIDE):
        for z in range(SIDE):
            for core in range(CORES):
                to = ((x + step) % SIDE, z) if core == order else (x, (z + step) % SIDE)
                route.append(((x * SIDE + z) * CORES + core, (to[0] * SIDE + to[1]) * CORES + core))
    return lax.ppermute(block, ("x", "z", "core"), route)


def join(blocks):
    def kernel(*refs):
        at = 0
        for ref in refs[:-1]:
            refs[-1][at : at + ref.shape[0]] = ref[...]
            at += ref.shape[0]

    total = sum(block.shape[0] for block in blocks)
    joined = jax.ShapeDtypeStruct((total, *blocks[0].shape[1:]), blocks[0].dtype)
    size = joined.size * joined.dtype.itemsize
    return pl.pallas_call(
        kernel,
        out_shape=joined,
        in_specs=[VMEM] * len(blocks),
        out_specs=VMEM,
        compiler_params=pltpu.CompilerParams(vmem_limit_bytes=2 * size + (1 << 18)),
        cost_estimate=pl.CostEstimate(flops=0, bytes_accessed=2 * size, transcendentals=0),
        name="join",
    )(*blocks)


def pack_kernel(count_ref, terms_ref, *refs):
    mine_refs, theirs_ref, rows_ref, windows = refs[:SIDE], refs[-3], refs[-2], refs[-1]
    slots, orbitals, basis = terms_ref.shape
    columns = basis // SIDE
    chip_rows = rows_ref.shape[2]
    y, core = lax.axis_index("y"), lax.axis_index("core")
    for s in range(slots):
        live = s < count_ref[y]
        at = pl.ds(s * orbitals, orbitals)
        for p in range(SIDE):
            for q in range(CORES):
                start = p * columns + q * WIDE
                width = min(WIDE, basis - start)
                block = terms_ref[s, :, start : start + width]
                windows[p * CORES + q, at, :width] = jnp.where(live, block, jnp.zeros_like(block))
                if width < WIDE:
                    windows[p * CORES + q, at, width:] = jnp.zeros((orbitals, WIDE - width), block.dtype)
        for i in range(PLANE):
            block = terms_ref[s, :, i * chip_rows : (i + 1) * chip_rows]
            rows_ref[i, at, :] = jnp.where(live, block, jnp.zeros_like(block))
    for dy in range(SIDE):
        plane = lax.rem(y + dy, SIDE) * CORES
        mine_refs[dy][...] = windows[plane + core]
        theirs_ref[dy] = windows[plane + 1 - core]


def pack(counts, terms):
    slots, orbitals, basis = terms.shape
    depth = slots * orbitals
    window = jax.ShapeDtypeStruct((depth, WIDE), terms.dtype)
    other_windows = jax.ShapeDtypeStruct((SIDE, depth, WIDE), terms.dtype)
    chip_rows = jax.ShapeDtypeStruct((PLANE, depth, basis // PLANE), terms.dtype)
    *mine, theirs, rows = pl.pallas_call(
        pack_kernel,
        out_shape=(window,) * SIDE + (other_windows, chip_rows),
        in_specs=[SMEM, VMEM],
        out_specs=(VMEM,) * (SIDE + 2),
        scratch_shapes=[pltpu.VMEM((CORES * SIDE, depth, WIDE), terms.dtype)],
        compiler_params=pltpu.CompilerParams(vmem_limit_bytes=10 << 20),
        name="pack",
    )(counts, terms)
    return mine, theirs, rows


def pair_kernel(*refs):
    mine_refs, got_ref, out_refs = refs[:SIDE], refs[SIDE], refs[SIDE + 1 :]
    depth = got_ref.shape[1]
    for dy in range(SIDE):
        out_refs[dy][:depth, :] = mine_refs[dy][...]
        out_refs[dy][depth:, :] = got_ref[dy]


def pair(mine, got):
    window = jax.ShapeDtypeStruct((CORES * got.shape[1], WIDE), got.dtype)
    return pl.pallas_call(
        pair_kernel,
        out_shape=(window,) * SIDE,
        in_specs=[VMEM] * (SIDE + 1),
        out_specs=(VMEM,) * SIDE,
        compiler_params=pltpu.CompilerParams(vmem_limit_bytes=6 << 20),
        name="pair",
    )(*mine, got)


OWN = tuple((dcore, 0) for dcore in range(CORES))
OTHERS = tuple((dcore, dy) for dy in range(1, SIDE) for dcore in range(CORES))


def at(v, *us):
    return tuple((u, v) for u in us)


def gathered_briefly(own):
    before, after = along_plane(own, 0, 1), along_plane(own, 0, -1)
    far = along_plane(before, 0, 1)
    line = join([own, before, after, far])
    left, right = along_plane(line, 1, 1), along_plane(line, 1, -1)
    cut = line.shape[0] // 2
    opposite = along_plane(left[:cut], 1, 1), along_plane(right[cut:], 1, -1)
    offsets = at(0, 0, -1, 1, 2) + at(-1, 0, -1, 1, 2) + at(1, 0, -1, 1, 2) + at(2, 0, -1, 1, 2)
    return offsets, (line, left, right, *opposite)


def gathered(own):
    cut = own.shape[0] // 2
    before, after = along_plane(own, 0, 1), along_plane(own, 0, -1)
    near = join([before, after])
    own_sides = along_plane(own, 1, 1), along_plane(own, 1, -1)
    near_sides = along_plane(near, 1, 1), along_plane(near, 1, -1)
    far = along_plane(before, 0, 1)
    far_sides = along_plane(far, 1, 1), along_plane(far, 1, -1)
    own_opposite = along_plane(own_sides[0], 1, 1)
    near_opposite = along_plane(near_sides[0][:cut], 1, 1), along_plane(near_sides[1][cut:], 1, -1)
    far_opposite = along_plane(far_sides[1], 1, -1)

    parts = [(at(0, 0), 0, own), (at(0, -1, 1), 0, near), (at(0, 2), 0, far)]
    parts += [(at(v, 0), 0, block) for v, block in zip((-1, 1), own_sides)]
    parts += [(at(v, -1, 1), 0, block) for v, block in zip((-1, 1), near_sides)]
    parts += [(at(2, 0), 0, own_opposite)]
    parts += [(at(v, 2), 0, block) for v, block in zip((-1, 1), far_sides)]
    parts += [(at(2, -1, 1), 0, near_opposite[0]), (at(2, -1, 1), len(OTHERS) // 2, near_opposite[1])]
    parts += [(at(2, 2), 0, far_opposite)]
    return parts


def arrange_kernel(layout, *refs):
    in_refs, out_refs = refs[: -len(layout)], refs[-len(layout) :]
    depth = in_refs[0].shape[1]
    x, z, core = (lax.axis_index(name) for name in ("x", "z", "core"))
    for blocks, out_ref in zip(layout, out_refs):
        for i, (u, v, dcore, place) in enumerate(blocks):
            dx, dz = jnp.where(core == 0, u, v), jnp.where(core == 0, v, u)
            chip = lax.rem(x + dx + SIDE, SIDE) * SIDE + lax.rem(z + dz + SIDE, SIDE)
            out_ref[i * depth : (i + 1) * depth, :] = in_refs[dcore][place * PLANE + chip]


def arrange(layout, *rows):
    depth, chip_rows = rows[0].shape[1:]
    size = sum(map(len, layout)) * depth * chip_rows * rows[0].dtype.itemsize
    return pl.pallas_call(
        lambda *refs: arrange_kernel(layout, *refs),
        out_shape=tuple(jax.ShapeDtypeStruct((len(blocks) * depth, chip_rows), rows[0].dtype) for blocks in layout),
        in_specs=[VMEM] * CORES,
        out_specs=(VMEM,) * len(layout),
        compiler_params=pltpu.CompilerParams(vmem_limit_bytes=2 * size + (1 << 20)),
        cost_estimate=pl.CostEstimate(flops=0, bytes_accessed=2 * size, transcendentals=0),
        name="arrange",
    )(*rows)


def halve_kernel(tile_ref, kept_ref, sent_ref):
    rows = kept_ref.shape[0]
    for core in range(CORES):

        @pl.when(lax.axis_index("core") == core)
        def _():
            kept_ref[...] = tile_ref[core * rows : (core + 1) * rows, :]
            sent_ref[...] = tile_ref[(1 - core) * rows : (2 - core) * rows, :]


def halve(tile):
    half = jax.ShapeDtypeStruct((tile.shape[0] // CORES, tile.shape[1]), tile.dtype)
    return pl.pallas_call(
        halve_kernel,
        out_shape=(half, half),
        in_specs=[VMEM],
        out_specs=(VMEM, VMEM),
        compiler_params=pltpu.CompilerParams(vmem_limit_bytes=8 << 20),
        name="halve",
    )(tile)


def assemble_kernel(kept_ref, got_ref, out_ref):
    rest = out_ref.shape[1] - WIDE
    for core in range(CORES):

        @pl.when(lax.axis_index("core") == core)
        def _():
            first, last = (kept_ref, got_ref) if core == 0 else (got_ref, kept_ref)
            out_ref[:, :WIDE] = first[...]
            out_ref[:, WIDE:] = last[:, :rest]


def assemble(kept, got, columns):
    return pl.pallas_call(
        assemble_kernel,
        out_shape=jax.ShapeDtypeStruct((got.shape[0], columns), got.dtype),
        in_specs=[VMEM, VMEM],
        out_specs=VMEM,
        compiler_params=pltpu.CompilerParams(vmem_limit_bytes=8 << 20),
        name="assemble",
    )(kept, got)


def body(b_tensor, aux_counts):
    basis = b_tensor.shape[0]
    mine, theirs, rows = pack(aux_counts, b_tensor.transpose(1, 2, 0))

    got = swap_cores(theirs)
    windows = pair(mine, got)
    others = join([along_y(windows[-dy % SIDE], -dy % SIDE) for dy in range(1, SIDE)])
    rows = lax.all_to_all(rows, ("x", "z"), 0, 0, tiled=True)
    offsets, early = gathered_briefly(windows[0])
    parts = gathered(others)

    left, right = along_y(rows, 1), along_y(rows, -1)
    half = PLANE // 2
    far = along_y(left[:half], 1), along_y(right[half:], -1)
    rest = join([right, *far, left])
    other_rows = swap_cores(rows)
    other_rest = swap_cores(rest)

    def product(weight, block):
        return lax.dot_general(weight, block, (((0,), (0,)), ((), ())), preferred_element_type=jnp.float32)

    (weight,) = arrange([[(u, v, dcore, dy) for u, v in offsets for dcore, dy in OWN]], rows, other_rows)
    tile = product(weight, join(early))
    layout = []
    for offsets, skipped, block in parts:
        blocks = [(u, v, dcore, dy - 1) for u, v in offsets for dcore, dy in OTHERS]
        layout.append(blocks[skipped : skipped + block.shape[0] // rows.shape[1]])
    weights = arrange(layout, rest, other_rest)
    for (_, _, block), weight in zip(parts, weights):
        tile = lax.optimization_barrier(tile + product(weight, block))

    kept, sent = halve(tile)
    return assemble(kept, swap_cores(sent), basis // SIDE)


def solution(mesh):
    fine = Mesh(mesh.devices.reshape(SIDE, SIDE, SIDE, CORES), ("y", "x", "z", "core"))
    return jax.shard_map(
        body,
        mesh=fine,
        in_specs=(P(None, "y", ("x", "z", "core")), P()),
        out_specs=P(("x", "z", "core"), "y"),
        check_vma=False,
    )
```

```python
import jax
import jax.numpy as jnp
from jax import lax
from jax.experimental import pallas as pl
from jax.experimental.pallas import tpu as pltpu
from jax.sharding import Mesh, PartitionSpec as P


SIDE = 4
CORES = 2
PLANE = SIDE * SIDE
WIDE = 1280
VMEM = pl.BlockSpec(memory_space=pltpu.VMEM)
SMEM = pl.BlockSpec(memory_space=pltpu.SMEM)


def along_y(block, step):
    return lax.ppermute(block, "y", [(i, (i + step) % SIDE) for i in range(SIDE)])


def swap_cores(block):
    return lax.ppermute(block, "core", [(0, 1), (1, 0)])


def along_plane(block, order, step):
    route = []
    for x in range(SIDE):
        for z in range(SIDE):
            for core in range(CORES):
                to = ((x + step) % SIDE, z) if core == order else (x, (z + step) % SIDE)
                route.append(((x * SIDE + z) * CORES + core, (to[0] * SIDE + to[1]) * CORES + core))
    return lax.ppermute(block, ("x", "z", "core"), route)


def join(blocks):
    def kernel(*refs):
        at = 0
        for ref in refs[:-1]:
            refs[-1][at : at + ref.shape[0]] = ref[...]
            at += ref.shape[0]

    total = sum(block.shape[0] for block in blocks)
    joined = jax.ShapeDtypeStruct((total, *blocks[0].shape[1:]), blocks[0].dtype)
    size = joined.size * joined.dtype.itemsize
    return pl.pallas_call(
        kernel,
        out_shape=joined,
        in_specs=[VMEM] * len(blocks),
        out_specs=VMEM,
        compiler_params=pltpu.CompilerParams(vmem_limit_bytes=2 * size + (1 << 18)),
        cost_estimate=pl.CostEstimate(flops=0, bytes_accessed=2 * size, transcendentals=0),
        name="join",
    )(*blocks)


def pack_kernel(count_ref, terms_ref, *refs):
    mine_refs, theirs_ref, rows_ref, windows = refs[:SIDE], refs[-3], refs[-2], refs[-1]
    slots, orbitals, basis = terms_ref.shape
    columns = basis // SIDE
    chip_rows = rows_ref.shape[2]
    y, core = lax.axis_index("y"), lax.axis_index("core")
    for s in range(slots):
        live = s < count_ref[y]
        at = pl.ds(s * orbitals, orbitals)
        for p in range(SIDE):
            for q in range(CORES):
                start = p * columns + q * WIDE
                width = min(WIDE, basis - start)
                block = terms_ref[s, :, start : start + width]
                windows[p * CORES + q, at, :width] = jnp.where(live, block, jnp.zeros_like(block))
                if width < WIDE:
                    windows[p * CORES + q, at, width:] = jnp.zeros((orbitals, WIDE - width), block.dtype)
        for i in range(PLANE):
            block = terms_ref[s, :, i * chip_rows : (i + 1) * chip_rows]
            rows_ref[i, at, :] = jnp.where(live, block, jnp.zeros_like(block))
    for dy in range(SIDE):
        plane = lax.rem(y + dy, SIDE) * CORES
        mine_refs[dy][...] = windows[plane + core]
        theirs_ref[dy] = windows[plane + 1 - core]


def pack(counts, terms):
    slots, orbitals, basis = terms.shape
    depth = slots * orbitals
    window = jax.ShapeDtypeStruct((depth, WIDE), terms.dtype)
    other_windows = jax.ShapeDtypeStruct((SIDE, depth, WIDE), terms.dtype)
    chip_rows = jax.ShapeDtypeStruct((PLANE, depth, basis // PLANE), terms.dtype)
    *mine, theirs, rows = pl.pallas_call(
        pack_kernel,
        out_shape=(window,) * SIDE + (other_windows, chip_rows),
        in_specs=[SMEM, VMEM],
        out_specs=(VMEM,) * (SIDE + 2),
        scratch_shapes=[pltpu.VMEM((CORES * SIDE, depth, WIDE), terms.dtype)],
        compiler_params=pltpu.CompilerParams(vmem_limit_bytes=10 << 20),
        name="pack",
    )(counts, terms)
    return mine, theirs, rows


def pair_kernel(*refs):
    mine_refs, got_ref, out_refs = refs[:SIDE], refs[SIDE], refs[SIDE + 1 :]
    depth = got_ref.shape[1]
    for dy in range(SIDE):
        out_refs[dy][:depth, :] = mine_refs[dy][...]
        out_refs[dy][depth:, :] = got_ref[dy]


def pair(mine, got):
    window = jax.ShapeDtypeStruct((CORES * got.shape[1], WIDE), got.dtype)
    return pl.pallas_call(
        pair_kernel,
        out_shape=(window,) * SIDE,
        in_specs=[VMEM] * (SIDE + 1),
        out_specs=(VMEM,) * SIDE,
        compiler_params=pltpu.CompilerParams(vmem_limit_bytes=6 << 20),
        name="pair",
    )(*mine, got)


OWN = tuple((dcore, 0) for dcore in range(CORES))
OTHERS = tuple((dcore, dy) for dy in range(1, SIDE) for dcore in range(CORES))


def at(v, *us):
    return tuple((u, v) for u in us)


def gathered_briefly(own):
    before, after, far = (along_plane(own, 0, step) for step in (1, -1, 2))
    line = join([own, before, after, far])
    left, right = along_plane(line, 1, 1), along_plane(line, 1, -1)
    cut = line.shape[0] // 2
    opposite = along_plane(left[:cut], 1, 1), along_plane(right[cut:], 1, -1)
    offsets = at(0, 0, -1, 1, 2) + at(-1, 0, -1, 1, 2) + at(1, 0, -1, 1, 2) + at(2, 0, -1, 1, 2)
    return offsets, (line, left, right, *opposite)


def gathered(own):
    cut = own.shape[0] // 2
    before, after = along_plane(own, 0, 1), along_plane(own, 0, -1)
    near = join([before, after])
    own_sides = along_plane(own, 1, 1), along_plane(own, 1, -1)
    near_sides = along_plane(near, 1, 1), along_plane(near, 1, -1)
    far = along_plane(before, 0, 1)
    far_sides = along_plane(far, 1, 1), along_plane(far, 1, -1)
    own_opposite = along_plane(own_sides[0], 1, 1)
    near_opposite = along_plane(near_sides[0][:cut], 1, 1), along_plane(near_sides[1][cut:], 1, -1)
    far_opposite = along_plane(far_sides[1], 1, -1)

    parts = [(at(0, 0), 0, own), (at(0, -1, 1), 0, near), (at(0, 2), 0, far)]
    parts += [(at(v, 0), 0, block) for v, block in zip((-1, 1), own_sides)]
    parts += [(at(v, -1, 1), 0, block) for v, block in zip((-1, 1), near_sides)]
    parts += [(at(2, 0), 0, own_opposite)]
    parts += [(at(v, 2), 0, block) for v, block in zip((-1, 1), far_sides)]
    parts += [(at(2, -1, 1), 0, near_opposite[0]), (at(2, -1, 1), len(OTHERS) // 2, near_opposite[1])]
    parts += [(at(2, 2), 0, far_opposite)]
    return parts


def arrange_kernel(layout, *refs):
    in_refs, out_refs = refs[: -len(layout)], refs[-len(layout) :]
    depth = in_refs[0].shape[1]
    x, z, core = (lax.axis_index(name) for name in ("x", "z", "core"))
    for blocks, out_ref in zip(layout, out_refs):
        for i, (u, v, dcore, place) in enumerate(blocks):
            dx, dz = jnp.where(core == 0, u, v), jnp.where(core == 0, v, u)
            chip = lax.rem(x + dx + SIDE, SIDE) * SIDE + lax.rem(z + dz + SIDE, SIDE)
            out_ref[i * depth : (i + 1) * depth, :] = in_refs[dcore][place * PLANE + chip]


def arrange(layout, *rows):
    depth, chip_rows = rows[0].shape[1:]
    size = sum(map(len, layout)) * depth * chip_rows * rows[0].dtype.itemsize
    return pl.pallas_call(
        lambda *refs: arrange_kernel(layout, *refs),
        out_shape=tuple(jax.ShapeDtypeStruct((len(blocks) * depth, chip_rows), rows[0].dtype) for blocks in layout),
        in_specs=[VMEM] * CORES,
        out_specs=(VMEM,) * len(layout),
        compiler_params=pltpu.CompilerParams(vmem_limit_bytes=2 * size + (1 << 20)),
        cost_estimate=pl.CostEstimate(flops=0, bytes_accessed=2 * size, transcendentals=0),
        name="arrange",
    )(*rows)


def halve_kernel(tile_ref, kept_ref, sent_ref):
    rows = kept_ref.shape[0]
    for core in range(CORES):

        @pl.when(lax.axis_index("core") == core)
        def _():
            kept_ref[...] = tile_ref[core * rows : (core + 1) * rows, :]
            sent_ref[...] = tile_ref[(1 - core) * rows : (2 - core) * rows, :]


def halve(tile):
    half = jax.ShapeDtypeStruct((tile.shape[0] // CORES, tile.shape[1]), tile.dtype)
    return pl.pallas_call(
        halve_kernel,
        out_shape=(half, half),
        in_specs=[VMEM],
        out_specs=(VMEM, VMEM),
        compiler_params=pltpu.CompilerParams(vmem_limit_bytes=8 << 20),
        name="halve",
    )(tile)


def assemble_kernel(kept_ref, got_ref, out_ref):
    rest = out_ref.shape[1] - WIDE
    for core in range(CORES):

        @pl.when(lax.axis_index("core") == core)
        def _():
            first, last = (kept_ref, got_ref) if core == 0 else (got_ref, kept_ref)
            out_ref[:, :WIDE] = first[...]
            out_ref[:, WIDE:] = last[:, :rest]


def assemble(kept, got, columns):
    return pl.pallas_call(
        assemble_kernel,
        out_shape=jax.ShapeDtypeStruct((got.shape[0], columns), got.dtype),
        in_specs=[VMEM, VMEM],
        out_specs=VMEM,
        compiler_params=pltpu.CompilerParams(vmem_limit_bytes=8 << 20),
        name="assemble",
    )(kept, got)


def body(b_tensor, aux_counts):
    basis = b_tensor.shape[0]
    mine, theirs, rows = pack(aux_counts, b_tensor.transpose(1, 2, 0))

    got = swap_cores(theirs)
    windows = pair(mine, got)
    others = join([along_y(windows[-dy % SIDE], -dy % SIDE) for dy in range(1, SIDE)])
    rows = lax.all_to_all(rows, ("x", "z"), 0, 0, tiled=True)
    offsets, early = gathered_briefly(windows[0])
    parts = gathered(others)

    left, right = along_y(rows, 1), along_y(rows, -1)
    half = PLANE // 2
    far = along_y(left[:half], 1), along_y(right[half:], -1)
    rest = join([right, *far, left])
    other_rows = swap_cores(rows)
    other_rest = swap_cores(rest)

    def product(weight, block):
        return lax.dot_general(weight, block, (((0,), (0,)), ((), ())), preferred_element_type=jnp.float32)

    (weight,) = arrange([[(u, v, dcore, dy) for u, v in offsets for dcore, dy in OWN]], rows, other_rows)
    early = join(early)
    tile = product(weight, early)
    layout = []
    for offsets, skipped, block in parts:
        blocks = [(u, v, dcore, dy - 1) for u, v in offsets for dcore, dy in OTHERS]
        layout.append(blocks[skipped : skipped + block.shape[0] // rows.shape[1]])
    weights = arrange(layout, rest, other_rest)
    for (_, _, block), weight in zip(parts, weights):
        tile = lax.optimization_barrier(tile + product(weight, block))

    kept, sent = halve(tile)
    return assemble(kept, swap_cores(sent), basis // SIDE)


def solution(mesh):
    fine = Mesh(mesh.devices.reshape(SIDE, SIDE, SIDE, CORES), ("y", "x", "z", "core"))
    return jax.shard_map(
        body,
        mesh=fine,
        in_specs=(P(None, "y", ("x", "z", "core")), P()),
        out_specs=P(("x", "z", "core"), "y"),
        check_vma=False,
    )
```

```python
import jax
import jax.numpy as jnp
from jax import lax
from jax.experimental import pallas as pl
from jax.experimental.pallas import tpu as pltpu
from jax.sharding import Mesh, PartitionSpec as P


SIDE = 4
CORES = 2
PLANE = SIDE * SIDE
WIDE = 1280
VMEM = pl.BlockSpec(memory_space=pltpu.VMEM)
SMEM = pl.BlockSpec(memory_space=pltpu.SMEM)


def along_y(block, step):
    return lax.ppermute(block, "y", [(i, (i + step) % SIDE) for i in range(SIDE)])


def swap_cores(block):
    return lax.ppermute(block, "core", [(0, 1), (1, 0)])


def along_plane(block, order, step):
    route = []
    for x in range(SIDE):
        for z in range(SIDE):
            for core in range(CORES):
                to = ((x + step) % SIDE, z) if core == order else (x, (z + step) % SIDE)
                route.append(((x * SIDE + z) * CORES + core, (to[0] * SIDE + to[1]) * CORES + core))
    return lax.ppermute(block, ("x", "z", "core"), route)


def join(blocks):
    def kernel(*refs):
        at = 0
        for ref in refs[:-1]:
            refs[-1][at : at + ref.shape[0]] = ref[...]
            at += ref.shape[0]

    total = sum(block.shape[0] for block in blocks)
    joined = jax.ShapeDtypeStruct((total, *blocks[0].shape[1:]), blocks[0].dtype)
    size = joined.size * joined.dtype.itemsize
    return pl.pallas_call(
        kernel,
        out_shape=joined,
        in_specs=[VMEM] * len(blocks),
        out_specs=VMEM,
        compiler_params=pltpu.CompilerParams(vmem_limit_bytes=2 * size + (1 << 18)),
        cost_estimate=pl.CostEstimate(flops=0, bytes_accessed=2 * size, transcendentals=0),
        name="join",
    )(*blocks)


def pack_kernel(count_ref, terms_ref, *refs):
    mine_refs, theirs_ref, rows_refs, (windows, rows) = refs[:SIDE], refs[SIDE], refs[SIDE + 1 : -2], refs[-2:]
    slots, orbitals, basis = terms_ref.shape
    columns = basis // SIDE
    chip_rows = rows.shape[2]
    x, y, z, core = (lax.axis_index(name) for name in ("x", "y", "z", "core"))
    for s in range(slots):
        live = s < count_ref[y]
        at = pl.ds(s * orbitals, orbitals)
        for p in range(SIDE):
            for q in range(CORES):
                start = p * columns + q * WIDE
                width = min(WIDE, basis - start)
                block = terms_ref[s, :, start : start + width]
                windows[p * CORES + q, at, :width] = jnp.where(live, block, jnp.zeros_like(block))
                if width < WIDE:
                    windows[p * CORES + q, at, width:] = jnp.zeros((orbitals, WIDE - width), block.dtype)
        for i in range(PLANE):
            block = terms_ref[s, :, i * chip_rows : (i + 1) * chip_rows]
            rows[i, at, :] = jnp.where(live, block, jnp.zeros_like(block))
    for dy in range(SIDE):
        plane = lax.rem(y + dy, SIDE) * CORES
        mine_refs[dy][...] = windows[plane + core]
        theirs_ref[dy] = windows[plane + 1 - core]
    for u, rows_ref in zip(OFFSETS, rows_refs):
        for i, v in enumerate(OFFSETS):
            dx, dz = jnp.where(core == 0, u, v), jnp.where(core == 0, v, u)
            rows_ref[i] = rows[lax.rem(x + dx + SIDE, SIDE) * SIDE + lax.rem(z + dz + SIDE, SIDE)]


def pack(counts, terms):
    slots, orbitals, basis = terms.shape
    depth = slots * orbitals
    window = jax.ShapeDtypeStruct((depth, WIDE), terms.dtype)
    other_windows = jax.ShapeDtypeStruct((SIDE, depth, WIDE), terms.dtype)
    line_rows = jax.ShapeDtypeStruct((SIDE, depth, basis // PLANE), terms.dtype)
    *mine, theirs, rows_0, rows_1, rows_2, rows_3 = pl.pallas_call(
        pack_kernel,
        out_shape=(window,) * SIDE + (other_windows,) + (line_rows,) * SIDE,
        in_specs=[SMEM, VMEM],
        out_specs=(VMEM,) * (2 * SIDE + 1),
        scratch_shapes=[
            pltpu.VMEM((CORES * SIDE, depth, WIDE), terms.dtype),
            pltpu.VMEM((PLANE, depth, basis // PLANE), terms.dtype),
        ],
        compiler_params=pltpu.CompilerParams(vmem_limit_bytes=12 << 20),
        name="pack",
    )(counts, terms)
    return mine, theirs, (rows_0, rows_1, rows_2, rows_3)


def regroup_kernel(*refs):
    for i, in_ref in enumerate(refs[:SIDE]):
        for j, out_ref in enumerate(refs[SIDE:]):
            out_ref[i] = in_ref[j]


def regroup(blocks):
    return pl.pallas_call(
        regroup_kernel,
        out_shape=tuple(jax.ShapeDtypeStruct(block.shape, block.dtype) for block in blocks),
        in_specs=[VMEM] * SIDE,
        out_specs=(VMEM,) * SIDE,
        compiler_params=pltpu.CompilerParams(vmem_limit_bytes=6 << 20),
        name="regroup",
    )(*blocks)


def along_line(blocks, order):
    got = {0: blocks[0]}
    for offset, block in zip(OFFSETS[1:], blocks[1:]):
        got[-offset if offset < 2 else 2] = along_plane(block, order, offset)
    return [got[offset] for offset in OFFSETS]


def pair_kernel(*refs):
    mine_refs, got_ref, out_refs = refs[:SIDE], refs[SIDE], refs[SIDE + 1 :]
    depth = got_ref.shape[1]
    for dy in range(SIDE):
        out_refs[dy][:depth, :] = mine_refs[dy][...]
        out_refs[dy][depth:, :] = got_ref[dy]


def pair(mine, got):
    window = jax.ShapeDtypeStruct((CORES * got.shape[1], WIDE), got.dtype)
    return pl.pallas_call(
        pair_kernel,
        out_shape=(window,) * SIDE,
        in_specs=[VMEM] * (SIDE + 1),
        out_specs=(VMEM,) * SIDE,
        compiler_params=pltpu.CompilerParams(vmem_limit_bytes=6 << 20),
        name="pair",
    )(*mine, got)


OFFSETS = (0, -1, 1, 2)
OWN = tuple((dcore, 0) for dcore in range(CORES))
OTHERS = tuple((dcore, dy) for dy in range(1, SIDE) for dcore in range(CORES))


def at(v, *us):
    return tuple((u, v) for u in us)


def gathered_briefly(own):
    before, after, far = (along_plane(own, 0, step) for step in (1, -1, 2))
    line = join([own, before, after, far])
    left, right = along_plane(line, 1, 1), along_plane(line, 1, -1)
    cut = line.shape[0] // 2
    opposite = along_plane(left[:cut], 1, 1), along_plane(right[cut:], 1, -1)
    first = sum((at(v, 0, -1, 1, 2) for v in (0, -1, 1)), ())
    last = join(opposite)
    return (first, join([line, left, right])), (at(2, 0, -1, 1, 2), last)


def gathered(own):
    cut = own.shape[0] // 2
    before, after = along_plane(own, 0, 1), along_plane(own, 0, -1)
    near = join([before, after])
    far = along_plane(before, 0, 1)
    near_sides = along_plane(near, 1, 1), along_plane(near, 1, -1)
    own_sides = along_plane(own, 1, 1), along_plane(own, 1, -1)
    far_sides = along_plane(far, 1, 1), along_plane(far, 1, -1)
    own_opposite = along_plane(own_sides[0], 1, 1)
    near_opposite = along_plane(near_sides[0][:cut], 1, 1), along_plane(near_sides[1][cut:], 1, -1)
    far_opposite = along_plane(far_sides[1], 1, -1)

    first = at(0, 0, -1, 1, 2) + at(-1, 0) + at(1, 0) + at(2, 0)
    parts = [(first, 0, join([own, near, far, *own_sides, own_opposite]))]
    parts += [(at(v, -1, 1), 0, block) for v, block in zip((-1, 1), near_sides)]
    parts += [(at(v, 2), 0, block) for v, block in zip((-1, 1), far_sides)]
    parts += [(at(2, -1, 1), 0, near_opposite[0]), (at(2, -1, 1), len(OTHERS) // 2, near_opposite[1])]
    parts += [(at(2, 2), 0, far_opposite)]
    return parts


def arrange_kernel(layout, *refs):
    in_refs, out_refs = refs[: -len(layout)], refs[-len(layout) :]
    depth = in_refs[0].shape[1]
    for blocks, out_ref in zip(layout, out_refs):
        for i, (u, v, dcore, place) in enumerate(blocks):
            first, second = (u, v) if dcore == 0 else (v, u)
            chip = OFFSETS.index(second) * SIDE + OFFSETS.index(first)
            out_ref[i * depth : (i + 1) * depth, :] = in_refs[dcore][place * PLANE + chip]


def arrange(layout, *rows):
    depth, chip_rows = rows[0].shape[1:]
    size = sum(map(len, layout)) * depth * chip_rows * rows[0].dtype.itemsize
    return pl.pallas_call(
        lambda *refs: arrange_kernel(layout, *refs),
        out_shape=tuple(jax.ShapeDtypeStruct((len(blocks) * depth, chip_rows), rows[0].dtype) for blocks in layout),
        in_specs=[VMEM] * CORES,
        out_specs=(VMEM,) * len(layout),
        compiler_params=pltpu.CompilerParams(vmem_limit_bytes=2 * size + (1 << 20)),
        cost_estimate=pl.CostEstimate(flops=0, bytes_accessed=2 * size, transcendentals=0),
        name="arrange",
    )(*rows)


def halve_kernel(tile_ref, kept_ref, sent_ref):
    rows = kept_ref.shape[0]
    for core in range(CORES):

        @pl.when(lax.axis_index("core") == core)
        def _():
            kept_ref[...] = tile_ref[core * rows : (core + 1) * rows, :]
            sent_ref[...] = tile_ref[(1 - core) * rows : (2 - core) * rows, :]


def halve(tile):
    half = jax.ShapeDtypeStruct((tile.shape[0] // CORES, tile.shape[1]), tile.dtype)
    return pl.pallas_call(
        halve_kernel,
        out_shape=(half, half),
        in_specs=[VMEM],
        out_specs=(VMEM, VMEM),
        compiler_params=pltpu.CompilerParams(vmem_limit_bytes=8 << 20),
        name="halve",
    )(tile)


def assemble_kernel(kept_ref, got_ref, out_ref):
    rest = out_ref.shape[1] - WIDE
    for core in range(CORES):

        @pl.when(lax.axis_index("core") == core)
        def _():
            first, last = (kept_ref, got_ref) if core == 0 else (got_ref, kept_ref)
            out_ref[:, :WIDE] = first[...]
            out_ref[:, WIDE:] = last[:, :rest]


def assemble(kept, got, columns):
    return pl.pallas_call(
        assemble_kernel,
        out_shape=jax.ShapeDtypeStruct((got.shape[0], columns), got.dtype),
        in_specs=[VMEM, VMEM],
        out_specs=VMEM,
        compiler_params=pltpu.CompilerParams(vmem_limit_bytes=8 << 20),
        name="assemble",
    )(kept, got)


def body(b_tensor, aux_counts):
    basis = b_tensor.shape[0]
    mine, theirs, rows = pack(aux_counts, b_tensor.transpose(1, 2, 0))

    got = swap_cores(theirs)
    windows = pair(mine, got)
    others = join([along_y(windows[-dy % SIDE], -dy % SIDE) for dy in range(1, SIDE)])
    rows = along_line(rows, 0)
    rows = regroup(rows)
    rows = along_line(rows, 1)
    rows = join(rows)
    early = gathered_briefly(windows[0])
    parts = gathered(others)

    left, right = along_y(rows, 1), along_y(rows, -1)
    half = PLANE // 2
    far = along_y(left[:half], 1), along_y(right[half:], -1)
    rest = join([right, *far, left])
    other_rows = swap_cores(rows)
    other_rest = swap_cores(rest)

    def product(weight, block):
        return lax.dot_general(weight, block, (((0,), (0,)), ((), ())), preferred_element_type=jnp.float32)

    layout = [[(u, v, dcore, dy) for u, v in offsets for dcore, dy in OWN] for offsets, _ in early]
    weights = arrange(layout, rows, other_rows)
    tile = product(weights[0], early[0][1])
    layout = []
    for offsets, skipped, block in parts:
        blocks = [(u, v, dcore, dy - 1) for u, v in offsets for dcore, dy in OTHERS]
        layout.append(blocks[skipped : skipped + block.shape[0] // rows.shape[1]])
    weights = (*arrange(layout, rest, other_rest), weights[1])
    blocks = [block for *_, block in parts] + [early[1][1]]
    for i in (0, 1, 2, len(parts), *range(3, len(parts))):
        tile = lax.optimization_barrier(tile + product(weights[i], blocks[i]))

    kept, sent = halve(tile)
    return assemble(kept, swap_cores(sent), basis // SIDE)


def solution(mesh):
    fine = Mesh(mesh.devices.reshape(SIDE, SIDE, SIDE, CORES), ("y", "x", "z", "core"))
    return jax.shard_map(
        body,
        mesh=fine,
        in_specs=(P(None, "y", ("x", "z", "core")), P()),
        out_specs=P(("x", "z", "core"), "y"),
        check_vma=False,
    )
```

```python
import jax
import jax.numpy as jnp
from jax import lax
from jax.experimental import pallas as pl
from jax.experimental.pallas import tpu as pltpu
from jax.sharding import Mesh, PartitionSpec as P


SIDE = 4
CORES = 2
PLANE = SIDE * SIDE
WIDE = 1280
VMEM = pl.BlockSpec(memory_space=pltpu.VMEM)
SMEM = pl.BlockSpec(memory_space=pltpu.SMEM)


def along_y(block, step):
    return lax.ppermute(block, "y", [(i, (i + step) % SIDE) for i in range(SIDE)])


def swap_cores(block):
    return lax.ppermute(block, "core", [(0, 1), (1, 0)])


def along_plane(block, order, step):
    route = []
    for x in range(SIDE):
        for z in range(SIDE):
            for core in range(CORES):
                to = ((x + step) % SIDE, z) if core == order else (x, (z + step) % SIDE)
                route.append(((x * SIDE + z) * CORES + core, (to[0] * SIDE + to[1]) * CORES + core))
    return lax.ppermute(block, ("x", "z", "core"), route)


def join(blocks):
    def kernel(*refs):
        at = 0
        for ref in refs[:-1]:
            refs[-1][at : at + ref.shape[0]] = ref[...]
            at += ref.shape[0]

    total = sum(block.shape[0] for block in blocks)
    joined = jax.ShapeDtypeStruct((total, *blocks[0].shape[1:]), blocks[0].dtype)
    size = joined.size * joined.dtype.itemsize
    return pl.pallas_call(
        kernel,
        out_shape=joined,
        in_specs=[VMEM] * len(blocks),
        out_specs=VMEM,
        compiler_params=pltpu.CompilerParams(vmem_limit_bytes=2 * size + (1 << 18)),
        cost_estimate=pl.CostEstimate(flops=0, bytes_accessed=2 * size, transcendentals=0),
        name="join",
    )(*blocks)


def pack_kernel(count_ref, terms_ref, *refs):
    mine_refs, theirs_ref, rows_refs, (windows, rows) = refs[:SIDE], refs[SIDE], refs[SIDE + 1 : -2], refs[-2:]
    slots, orbitals, basis = terms_ref.shape
    columns = basis // SIDE
    chip_rows = rows.shape[2]
    x, y, z, core = (lax.axis_index(name) for name in ("x", "y", "z", "core"))
    for s in range(slots):
        live = s < count_ref[y]
        at = pl.ds(s * orbitals, orbitals)
        for p in range(SIDE):
            for q in range(CORES):
                start = p * columns + q * WIDE
                width = min(WIDE, basis - start)
                block = terms_ref[s, :, start : start + width]
                windows[p * CORES + q, at, :width] = jnp.where(live, block, jnp.zeros_like(block))
                if width < WIDE:
                    windows[p * CORES + q, at, width:] = jnp.zeros((orbitals, WIDE - width), block.dtype)
        for i in range(PLANE):
            block = terms_ref[s, :, i * chip_rows : (i + 1) * chip_rows]
            rows[i, at, :] = jnp.where(live, block, jnp.zeros_like(block))
    for dy in range(SIDE):
        plane = lax.rem(y + dy, SIDE) * CORES
        mine_refs[dy][...] = windows[plane + core]
        theirs_ref[dy] = windows[plane + 1 - core]
    for u, rows_ref in zip(OFFSETS, rows_refs):
        for i, v in enumerate(OFFSETS):
            dx, dz = jnp.where(core == 0, u, v), jnp.where(core == 0, v, u)
            rows_ref[i] = rows[lax.rem(x + dx + SIDE, SIDE) * SIDE + lax.rem(z + dz + SIDE, SIDE)]


def pack(counts, terms):
    slots, orbitals, basis = terms.shape
    depth = slots * orbitals
    window = jax.ShapeDtypeStruct((depth, WIDE), terms.dtype)
    other_windows = jax.ShapeDtypeStruct((SIDE, depth, WIDE), terms.dtype)
    line_rows = jax.ShapeDtypeStruct((SIDE, depth, basis // PLANE), terms.dtype)
    *mine, theirs, rows_0, rows_1, rows_2, rows_3 = pl.pallas_call(
        pack_kernel,
        out_shape=(window,) * SIDE + (other_windows,) + (line_rows,) * SIDE,
        in_specs=[SMEM, VMEM],
        out_specs=(VMEM,) * (2 * SIDE + 1),
        scratch_shapes=[
            pltpu.VMEM((CORES * SIDE, depth, WIDE), terms.dtype),
            pltpu.VMEM((PLANE, depth, basis // PLANE), terms.dtype),
        ],
        compiler_params=pltpu.CompilerParams(vmem_limit_bytes=12 << 20),
        name="pack",
    )(counts, terms)
    return mine, theirs, (rows_0, rows_1, rows_2, rows_3)


def regroup_kernel(*refs):
    for i, in_ref in enumerate(refs[:SIDE]):
        for j, out_ref in enumerate(refs[SIDE:]):
            out_ref[i] = in_ref[j]


def regroup(blocks):
    return pl.pallas_call(
        regroup_kernel,
        out_shape=tuple(jax.ShapeDtypeStruct(block.shape, block.dtype) for block in blocks),
        in_specs=[VMEM] * SIDE,
        out_specs=(VMEM,) * SIDE,
        compiler_params=pltpu.CompilerParams(vmem_limit_bytes=6 << 20),
        name="regroup",
    )(*blocks)


def along_line(blocks, order):
    got = {0: blocks[0]}
    for offset, block in zip(OFFSETS[1:], blocks[1:]):
        got[-offset if offset < 2 else 2] = along_plane(block, order, offset)
    return [got[offset] for offset in OFFSETS]


def pair_kernel(*refs):
    mine_refs, got_ref, out_refs = refs[:SIDE], refs[SIDE], refs[SIDE + 1 :]
    depth = got_ref.shape[1]
    for dy in range(SIDE):
        out_refs[dy][:depth, :] = mine_refs[dy][...]
        out_refs[dy][depth:, :] = got_ref[dy]


def pair(mine, got):
    window = jax.ShapeDtypeStruct((CORES * got.shape[1], WIDE), got.dtype)
    return pl.pallas_call(
        pair_kernel,
        out_shape=(window,) * SIDE,
        in_specs=[VMEM] * (SIDE + 1),
        out_specs=(VMEM,) * SIDE,
        compiler_params=pltpu.CompilerParams(vmem_limit_bytes=6 << 20),
        name="pair",
    )(*mine, got)


OFFSETS = (0, -1, 1, 2)
OWN = tuple((dcore, 0) for dcore in range(CORES))
OTHERS = tuple((dcore, dy) for dy in range(1, SIDE) for dcore in range(CORES))


def at(v, *us):
    return tuple((u, v) for u in us)


def gathered_briefly(own):
    before, after, far = (along_plane(own, 0, step) for step in (1, -1, 2))
    line = join([own, before, after, far])
    left, right = along_plane(line, 1, 1), along_plane(line, 1, -1)
    cut = line.shape[0] // 2
    opposite = along_plane(left[:cut], 1, 1), along_plane(right[cut:], 1, -1)
    first = sum((at(v, 0, -1, 1, 2) for v in (0, -1, 1)), ())
    last = join(opposite)
    return (first, join([line, left, right])), (at(2, 0, -1, 1, 2), last)


def gathered(own):
    cut = own.shape[0] // 2
    before, after = along_plane(own, 0, 1), along_plane(own, 0, -1)
    near = join([before, after])
    far = along_plane(before, 0, 1)
    near_sides = along_plane(near, 1, 1), along_plane(near, 1, -1)
    own_sides = along_plane(own, 1, 1), along_plane(own, 1, -1)
    far_sides = along_plane(far, 1, 1), along_plane(far, 1, -1)
    own_opposite = along_plane(own_sides[0], 1, 1)
    near_opposite = along_plane(near_sides[0][:cut], 1, 1), along_plane(near_sides[1][cut:], 1, -1)
    far_opposite = along_plane(far_sides[1], 1, -1)

    first = at(0, 0, -1, 1, 2) + at(-1, 0) + at(1, 0)
    parts = [(first, 0, join([own, near, far, *own_sides]))]
    parts += [(at(v, -1, 1), 0, block) for v, block in zip((-1, 1), near_sides)]
    parts += [(at(-1, 2) + at(1, 2) + at(2, 0), 0, join([*far_sides, own_opposite]))]
    parts += [(at(2, -1, 1), 0, near_opposite[0]), (at(2, -1, 1), len(OTHERS) // 2, near_opposite[1])]
    parts += [(at(2, 2), 0, far_opposite)]
    return parts


def arrange_kernel(layout, *refs):
    in_refs, out_refs = refs[: -len(layout)], refs[-len(layout) :]
    depth = in_refs[0].shape[1]
    for blocks, out_ref in zip(layout, out_refs):
        for i, (u, v, dcore, place) in enumerate(blocks):
            first, second = (u, v) if dcore == 0 else (v, u)
            chip = OFFSETS.index(second) * SIDE + OFFSETS.index(first)
            out_ref[i * depth : (i + 1) * depth, :] = in_refs[dcore][place * PLANE + chip]


def arrange(layout, *rows):
    depth, chip_rows = rows[0].shape[1:]
    size = sum(map(len, layout)) * depth * chip_rows * rows[0].dtype.itemsize
    return pl.pallas_call(
        lambda *refs: arrange_kernel(layout, *refs),
        out_shape=tuple(jax.ShapeDtypeStruct((len(blocks) * depth, chip_rows), rows[0].dtype) for blocks in layout),
        in_specs=[VMEM] * CORES,
        out_specs=(VMEM,) * len(layout),
        compiler_params=pltpu.CompilerParams(vmem_limit_bytes=2 * size + (1 << 20)),
        cost_estimate=pl.CostEstimate(flops=0, bytes_accessed=2 * size, transcendentals=0),
        name="arrange",
    )(*rows)


def halve_kernel(tile_ref, kept_ref, sent_ref):
    rows = kept_ref.shape[0]
    for core in range(CORES):

        @pl.when(lax.axis_index("core") == core)
        def _():
            kept_ref[...] = tile_ref[core * rows : (core + 1) * rows, :]
            sent_ref[...] = tile_ref[(1 - core) * rows : (2 - core) * rows, :]


def halve(tile):
    half = jax.ShapeDtypeStruct((tile.shape[0] // CORES, tile.shape[1]), tile.dtype)
    return pl.pallas_call(
        halve_kernel,
        out_shape=(half, half),
        in_specs=[VMEM],
        out_specs=(VMEM, VMEM),
        compiler_params=pltpu.CompilerParams(vmem_limit_bytes=8 << 20),
        name="halve",
    )(tile)


def assemble_kernel(kept_ref, got_ref, out_ref):
    rest = out_ref.shape[1] - WIDE
    for core in range(CORES):

        @pl.when(lax.axis_index("core") == core)
        def _():
            first, last = (kept_ref, got_ref) if core == 0 else (got_ref, kept_ref)
            out_ref[:, :WIDE] = first[...]
            out_ref[:, WIDE:] = last[:, :rest]


def assemble(kept, got, columns):
    return pl.pallas_call(
        assemble_kernel,
        out_shape=jax.ShapeDtypeStruct((got.shape[0], columns), got.dtype),
        in_specs=[VMEM, VMEM],
        out_specs=VMEM,
        compiler_params=pltpu.CompilerParams(vmem_limit_bytes=8 << 20),
        name="assemble",
    )(kept, got)


def body(b_tensor, aux_counts):
    basis = b_tensor.shape[0]
    mine, theirs, rows = pack(aux_counts, b_tensor.transpose(1, 2, 0))

    got = swap_cores(theirs)
    windows = pair(mine, got)
    others = join([along_y(windows[-dy % SIDE], -dy % SIDE) for dy in range(1, SIDE)])
    rows = along_line(rows, 0)
    rows = regroup(rows)
    rows = along_line(rows, 1)
    rows = join(rows)
    early = gathered_briefly(windows[0])
    parts = gathered(others)

    left, right = along_y(rows, 1), along_y(rows, -1)
    half = PLANE // 2
    far = along_y(left[:half], 1), along_y(right[half:], -1)
    rest = join([right, *far, left])
    other_rows = swap_cores(rows)
    other_rest = swap_cores(rest)

    def product(weight, block):
        return lax.dot_general(weight, block, (((0,), (0,)), ((), ())), preferred_element_type=jnp.float32)

    layout = [[(u, v, dcore, dy) for u, v in offsets for dcore, dy in OWN] for offsets, _ in early]
    weights = arrange(layout, rows, other_rows)
    tile = product(weights[0], early[0][1])
    layout = []
    for offsets, skipped, block in parts:
        blocks = [(u, v, dcore, dy - 1) for u, v in offsets for dcore, dy in OTHERS]
        layout.append(blocks[skipped : skipped + block.shape[0] // rows.shape[1]])
    weights = (*arrange(layout, rest, other_rest), weights[1])
    blocks = [block for *_, block in parts] + [early[1][1]]
    for i in (1, 2, len(parts), 0, 4, 5, 3, *range(6, len(parts))):
        tile = lax.optimization_barrier(tile + product(weights[i], blocks[i]))

    kept, sent = halve(tile)
    return assemble(kept, swap_cores(sent), basis // SIDE)


def solution(mesh):
    fine = Mesh(mesh.devices.reshape(SIDE, SIDE, SIDE, CORES), ("y", "x", "z", "core"))
    return jax.shard_map(
        body,
        mesh=fine,
        in_specs=(P(None, "y", ("x", "z", "core")), P()),
        out_specs=P(("x", "z", "core"), "y"),
        check_vma=False,
    )
```

```python
import jax
import jax.numpy as jnp
from jax import lax
from jax.experimental import pallas as pl
from jax.experimental.pallas import tpu as pltpu
from jax.sharding import Mesh, PartitionSpec as P


SIDE = 4
CORES = 2
PLANE = SIDE * SIDE
WIDE = 1280
VMEM = pl.BlockSpec(memory_space=pltpu.VMEM)
SMEM = pl.BlockSpec(memory_space=pltpu.SMEM)


def along_y(block, step):
    return lax.ppermute(block, "y", [(i, (i + step) % SIDE) for i in range(SIDE)])


def swap_cores(block):
    return lax.ppermute(block, "core", [(0, 1), (1, 0)])


def along_plane(block, order, step):
    route = []
    for x in range(SIDE):
        for z in range(SIDE):
            for core in range(CORES):
                to = ((x + step) % SIDE, z) if core == order else (x, (z + step) % SIDE)
                route.append(((x * SIDE + z) * CORES + core, (to[0] * SIDE + to[1]) * CORES + core))
    return lax.ppermute(block, ("x", "z", "core"), route)


def join(blocks):
    def kernel(*refs):
        at = 0
        for ref in refs[:-1]:
            refs[-1][at : at + ref.shape[0]] = ref[...]
            at += ref.shape[0]

    total = sum(block.shape[0] for block in blocks)
    joined = jax.ShapeDtypeStruct((total, *blocks[0].shape[1:]), blocks[0].dtype)
    size = joined.size * joined.dtype.itemsize
    return pl.pallas_call(
        kernel,
        out_shape=joined,
        in_specs=[VMEM] * len(blocks),
        out_specs=VMEM,
        compiler_params=pltpu.CompilerParams(vmem_limit_bytes=2 * size + (1 << 18)),
        cost_estimate=pl.CostEstimate(flops=0, bytes_accessed=2 * size, transcendentals=0),
        name="join",
    )(*blocks)


def pack_kernel(count_ref, terms_ref, *refs):
    mine_refs, theirs_ref, rows_refs, (windows, rows) = refs[:SIDE], refs[SIDE], refs[SIDE + 1 : -2], refs[-2:]
    slots, orbitals, basis = terms_ref.shape
    columns = basis // SIDE
    chip_rows = rows.shape[2]
    x, y, z, core = (lax.axis_index(name) for name in ("x", "y", "z", "core"))
    for s in range(slots):
        live = s < count_ref[y]
        at = pl.ds(s * orbitals, orbitals)
        for p in range(SIDE):
            for q in range(CORES):
                start = p * columns + q * WIDE
                width = min(WIDE, basis - start)
                block = terms_ref[s, :, start : start + width]
                windows[p * CORES + q, at, :width] = jnp.where(live, block, jnp.zeros_like(block))
                if width < WIDE:
                    windows[p * CORES + q, at, width:] = jnp.zeros((orbitals, WIDE - width), block.dtype)
        for i in range(PLANE):
            block = terms_ref[s, :, i * chip_rows : (i + 1) * chip_rows]
            rows[i, at, :] = jnp.where(live, block, jnp.zeros_like(block))
    for dy in range(SIDE):
        plane = lax.rem(y + dy, SIDE) * CORES
        mine_refs[dy][...] = windows[plane + core]
        theirs_ref[dy] = windows[plane + 1 - core]
    for u, rows_ref in zip(OFFSETS, rows_refs):
        for i, v in enumerate(OFFSETS):
            dx, dz = jnp.where(core == 0, u, v), jnp.where(core == 0, v, u)
            rows_ref[i] = rows[lax.rem(x + dx + SIDE, SIDE) * SIDE + lax.rem(z + dz + SIDE, SIDE)]


def pack(counts, terms):
    slots, orbitals, basis = terms.shape
    depth = slots * orbitals
    window = jax.ShapeDtypeStruct((depth, WIDE), terms.dtype)
    other_windows = jax.ShapeDtypeStruct((SIDE, depth, WIDE), terms.dtype)
    line_rows = jax.ShapeDtypeStruct((SIDE, depth, basis // PLANE), terms.dtype)
    *mine, theirs, rows_0, rows_1, rows_2, rows_3 = pl.pallas_call(
        pack_kernel,
        out_shape=(window,) * SIDE + (other_windows,) + (line_rows,) * SIDE,
        in_specs=[SMEM, VMEM],
        out_specs=(VMEM,) * (2 * SIDE + 1),
        scratch_shapes=[
            pltpu.VMEM((CORES * SIDE, depth, WIDE), terms.dtype),
            pltpu.VMEM((PLANE, depth, basis // PLANE), terms.dtype),
        ],
        compiler_params=pltpu.CompilerParams(vmem_limit_bytes=12 << 20),
        name="pack",
    )(counts, terms)
    return mine, theirs, (rows_0, rows_1, rows_2, rows_3)


def regroup_kernel(*refs):
    for i, in_ref in enumerate(refs[:SIDE]):
        for j, out_ref in enumerate(refs[SIDE:]):
            out_ref[i] = in_ref[j]


def regroup(blocks):
    return pl.pallas_call(
        regroup_kernel,
        out_shape=tuple(jax.ShapeDtypeStruct(block.shape, block.dtype) for block in blocks),
        in_specs=[VMEM] * SIDE,
        out_specs=(VMEM,) * SIDE,
        compiler_params=pltpu.CompilerParams(vmem_limit_bytes=6 << 20),
        name="regroup",
    )(*blocks)


def along_line(blocks, order):
    got = {0: blocks[0]}
    for offset, block in zip(OFFSETS[1:], blocks[1:]):
        got[-offset if offset < 2 else 2] = along_plane(block, order, offset)
    return [got[offset] for offset in OFFSETS]


def pair_kernel(*refs):
    mine_refs, got_ref, out_refs = refs[:SIDE], refs[SIDE], refs[SIDE + 1 :]
    depth = got_ref.shape[1]
    for dy in range(SIDE):
        out_refs[dy][:depth, :] = mine_refs[dy][...]
        out_refs[dy][depth:, :] = got_ref[dy]


def pair(mine, got):
    window = jax.ShapeDtypeStruct((CORES * got.shape[1], WIDE), got.dtype)
    return pl.pallas_call(
        pair_kernel,
        out_shape=(window,) * SIDE,
        in_specs=[VMEM] * (SIDE + 1),
        out_specs=(VMEM,) * SIDE,
        compiler_params=pltpu.CompilerParams(vmem_limit_bytes=6 << 20),
        name="pair",
    )(*mine, got)


OFFSETS = (0, -1, 1, 2)
OWN = tuple((dcore, 0) for dcore in range(CORES))
OTHERS = tuple((dcore, dy) for dy in range(1, SIDE) for dcore in range(CORES))


def at(v, *us):
    return tuple((u, v) for u in us)


def gathered_briefly(own):
    before, after, far = (along_plane(own, 0, step) for step in (1, -1, 2))
    line = join([own, before, after, far])
    left, right = along_plane(line, 1, 1), along_plane(line, 1, -1)
    cut = line.shape[0] // 2
    opposite = along_plane(left[:cut], 1, 1), along_plane(right[cut:], 1, -1)
    first = sum((at(v, 0, -1, 1, 2) for v in (0, -1, 1)), ())
    last = join(opposite)
    return (first, join([line, left, right])), (at(2, 0, -1, 1, 2), last)


def gathered(own):
    before, after, far = (along_plane(own, 0, step) for step in (1, -1, 2))
    near = join([before, after])
    near_sides = along_plane(near, 1, 1), along_plane(near, 1, -1)
    own_sides = along_plane(own, 1, 1), along_plane(own, 1, -1)
    far_sides = along_plane(far, 1, 1), along_plane(far, 1, -1)
    own_opposite = along_plane(own_sides[0], 1, 1)
    near_opposite = along_plane(near_sides[1], 1, -1)
    far_opposite = along_plane(far_sides[1], 1, -1)

    first = at(0, 0, -1, 1, 2) + at(-1, 0) + at(1, 0)
    parts = [(first, join([own, near, far, *own_sides]))]
    parts += [(at(v, -1, 1), block) for v, block in zip((-1, 1), near_sides)]
    parts += [(at(-1, 2) + at(1, 2) + at(2, 0), join([*far_sides, own_opposite]))]
    parts += [(at(2, -1, 1), near_opposite), (at(2, 2), far_opposite)]
    return parts


def arrange_kernel(layout, *refs):
    in_refs, out_refs = refs[: -len(layout)], refs[-len(layout) :]
    depth = in_refs[0].shape[1]
    for blocks, out_ref in zip(layout, out_refs):
        for i, (u, v, dcore, place) in enumerate(blocks):
            first, second = (u, v) if dcore == 0 else (v, u)
            chip = OFFSETS.index(second) * SIDE + OFFSETS.index(first)
            out_ref[i * depth : (i + 1) * depth, :] = in_refs[dcore][place * PLANE + chip]


def arrange(layout, *rows):
    depth, chip_rows = rows[0].shape[1:]
    size = sum(map(len, layout)) * depth * chip_rows * rows[0].dtype.itemsize
    return pl.pallas_call(
        lambda *refs: arrange_kernel(layout, *refs),
        out_shape=tuple(jax.ShapeDtypeStruct((len(blocks) * depth, chip_rows), rows[0].dtype) for blocks in layout),
        in_specs=[VMEM] * CORES,
        out_specs=(VMEM,) * len(layout),
        compiler_params=pltpu.CompilerParams(vmem_limit_bytes=2 * size + (1 << 20)),
        cost_estimate=pl.CostEstimate(flops=0, bytes_accessed=2 * size, transcendentals=0),
        name="arrange",
    )(*rows)


def halve_kernel(tile_ref, kept_ref, sent_ref):
    rows = kept_ref.shape[0]
    for core in range(CORES):

        @pl.when(lax.axis_index("core") == core)
        def _():
            kept_ref[...] = tile_ref[core * rows : (core + 1) * rows, :]
            sent_ref[...] = tile_ref[(1 - core) * rows : (2 - core) * rows, :]


def halve(tile):
    half = jax.ShapeDtypeStruct((tile.shape[0] // CORES, tile.shape[1]), tile.dtype)
    return pl.pallas_call(
        halve_kernel,
        out_shape=(half, half),
        in_specs=[VMEM],
        out_specs=(VMEM, VMEM),
        compiler_params=pltpu.CompilerParams(vmem_limit_bytes=8 << 20),
        name="halve",
    )(tile)


def assemble_kernel(kept_ref, got_ref, out_ref):
    rest = out_ref.shape[1] - WIDE
    for core in range(CORES):

        @pl.when(lax.axis_index("core") == core)
        def _():
            first, last = (kept_ref, got_ref) if core == 0 else (got_ref, kept_ref)
            out_ref[:, :WIDE] = first[...]
            out_ref[:, WIDE:] = last[:, :rest]


def assemble(kept, got, columns):
    return pl.pallas_call(
        assemble_kernel,
        out_shape=jax.ShapeDtypeStruct((got.shape[0], columns), got.dtype),
        in_specs=[VMEM, VMEM],
        out_specs=VMEM,
        compiler_params=pltpu.CompilerParams(vmem_limit_bytes=8 << 20),
        name="assemble",
    )(kept, got)


def body(b_tensor, aux_counts):
    basis = b_tensor.shape[0]
    mine, theirs, rows = pack(aux_counts, b_tensor.transpose(1, 2, 0))

    got = swap_cores(theirs)
    windows = pair(mine, got)
    others = join([along_y(windows[-dy % SIDE], -dy % SIDE) for dy in range(1, SIDE)])
    rows = along_line(rows, 0)
    rows = regroup(rows)
    rows = along_line(rows, 1)
    rows = join(rows)
    early = gathered_briefly(windows[0])
    parts = gathered(others)

    left, right = along_y(rows, 1), along_y(rows, -1)
    half = PLANE // 2
    far = along_y(left[:half], 1), along_y(right[half:], -1)
    rest = join([right, *far, left])
    other_rows = swap_cores(rows)
    other_rest = swap_cores(rest)

    def product(weight, block):
        return lax.dot_general(weight, block, (((0,), (0,)), ((), ())), preferred_element_type=jnp.float32)

    layout = [[(u, v, dcore, dy) for u, v in offsets for dcore, dy in OWN] for offsets, _ in early]
    weights = arrange(layout, rows, other_rows)
    tile = product(weights[0], early[0][1])
    layout = [[(u, v, dcore, dy - 1) for u, v in offsets for dcore, dy in OTHERS] for offsets, _ in parts]
    weights = (*arrange(layout, rest, other_rest), weights[1])
    blocks = [block for _, block in parts] + [early[1][1]]
    for i in (1, 2, len(parts), 0, 3, 4, 5):
        tile = lax.optimization_barrier(tile + product(weights[i], blocks[i]))

    kept, sent = halve(tile)
    return assemble(kept, swap_cores(sent), basis // SIDE)


def solution(mesh):
    fine = Mesh(mesh.devices.reshape(SIDE, SIDE, SIDE, CORES), ("y", "x", "z", "core"))
    return jax.shard_map(
        body,
        mesh=fine,
        in_specs=(P(None, "y", ("x", "z", "core")), P()),
        out_specs=P(("x", "z", "core"), "y"),
        check_vma=False,
    )
```

```python
import jax
import jax.numpy as jnp
from jax import lax
from jax.experimental import pallas as pl
from jax.experimental.pallas import tpu as pltpu
from jax.sharding import Mesh, PartitionSpec as P


SIDE = 4
CORES = 2
PLANE = SIDE * SIDE
WIDE = 1280
VMEM = pl.BlockSpec(memory_space=pltpu.VMEM)
SMEM = pl.BlockSpec(memory_space=pltpu.SMEM)


def along_y(block, step):
    return lax.ppermute(block, "y", [(i, (i + step) % SIDE) for i in range(SIDE)])


def swap_cores(block):
    return lax.ppermute(block, "core", [(0, 1), (1, 0)])


def along_plane(block, order, step):
    route = []
    for x in range(SIDE):
        for z in range(SIDE):
            for core in range(CORES):
                to = ((x + step) % SIDE, z) if core == order else (x, (z + step) % SIDE)
                route.append(((x * SIDE + z) * CORES + core, (to[0] * SIDE + to[1]) * CORES + core))
    return lax.ppermute(block, ("x", "z", "core"), route)


def join(blocks):
    def kernel(*refs):
        at = 0
        for ref in refs[:-1]:
            refs[-1][at : at + ref.shape[0]] = ref[...]
            at += ref.shape[0]

    total = sum(block.shape[0] for block in blocks)
    joined = jax.ShapeDtypeStruct((total, *blocks[0].shape[1:]), blocks[0].dtype)
    size = joined.size * joined.dtype.itemsize
    return pl.pallas_call(
        kernel,
        out_shape=joined,
        in_specs=[VMEM] * len(blocks),
        out_specs=VMEM,
        compiler_params=pltpu.CompilerParams(vmem_limit_bytes=2 * size + (1 << 18)),
        cost_estimate=pl.CostEstimate(flops=0, bytes_accessed=2 * size, transcendentals=0),
        name="join",
    )(*blocks)


def place_on_line(out_refs, u, i, block):
    if u == 2:
        out_refs[2 if i < SIDE // 2 else 1][SIDE + i % (SIDE // 2)] = block
    else:
        out_refs[OFFSETS.index(u)][i] = block


def pack_kernel(count_ref, terms_ref, *refs):
    mine_refs, theirs_ref, rows_refs, (windows, rows) = refs[:SIDE], refs[SIDE], refs[SIDE + 1 : -2], refs[-2:]
    slots, orbitals, basis = terms_ref.shape
    columns = basis // SIDE
    chip_rows = rows.shape[2]
    x, y, z, core = (lax.axis_index(name) for name in ("x", "y", "z", "core"))
    for s in range(slots):
        live = s < count_ref[y]
        at = pl.ds(s * orbitals, orbitals)
        for p in range(SIDE):
            for q in range(CORES):
                start = p * columns + q * WIDE
                width = min(WIDE, basis - start)
                block = terms_ref[s, :, start : start + width]
                windows[p * CORES + q, at, :width] = jnp.where(live, block, jnp.zeros_like(block))
                if width < WIDE:
                    windows[p * CORES + q, at, width:] = jnp.zeros((orbitals, WIDE - width), block.dtype)
        for i in range(PLANE):
            block = terms_ref[s, :, i * chip_rows : (i + 1) * chip_rows]
            rows[i, at, :] = jnp.where(live, block, jnp.zeros_like(block))
    for dy in range(SIDE):
        plane = lax.rem(y + dy, SIDE) * CORES
        mine_refs[dy][...] = windows[plane + core]
        theirs_ref[dy] = windows[plane + 1 - core]
    for u in OFFSETS:
        for i, v in enumerate(OFFSETS):
            dx, dz = jnp.where(core == 0, u, v), jnp.where(core == 0, v, u)
            block = rows[lax.rem(x + dx + SIDE, SIDE) * SIDE + lax.rem(z + dz + SIDE, SIDE)]
            place_on_line(rows_refs, u, i, block)


def pack(counts, terms):
    slots, orbitals, basis = terms.shape
    depth = slots * orbitals
    window = jax.ShapeDtypeStruct((depth, WIDE), terms.dtype)
    other_windows = jax.ShapeDtypeStruct((SIDE, depth, WIDE), terms.dtype)
    line_rows = line_shapes(depth, basis // PLANE, terms.dtype)
    *mine, theirs, kept, back, ahead = pl.pallas_call(
        pack_kernel,
        out_shape=(window,) * SIDE + (other_windows,) + line_rows,
        in_specs=[SMEM, VMEM],
        out_specs=(VMEM,) * (SIDE + 4),
        scratch_shapes=[
            pltpu.VMEM((CORES * SIDE, depth, WIDE), terms.dtype),
            pltpu.VMEM((PLANE, depth, basis // PLANE), terms.dtype),
        ],
        compiler_params=pltpu.CompilerParams(vmem_limit_bytes=12 << 20),
        name="pack",
    )(counts, terms)
    return mine, theirs, (kept, back, ahead)


def line_shapes(depth, chip_rows, dtype):
    return tuple(jax.ShapeDtypeStruct((n, depth, chip_rows), dtype) for n in (SIDE, SIDE + SIDE // 2, SIDE + SIDE // 2))


def by_sender(refs):
    kept, ahead, behind, far_behind, far_ahead = refs
    half = SIDE // 2
    return {
        0: [kept[i] for i in range(SIDE)],
        -1: [behind[i] for i in range(SIDE)],
        1: [ahead[i] for i in range(SIDE)],
        2: [far_behind[i] for i in range(half)] + [far_ahead[i] for i in range(half)],
    }


def regroup_kernel(*refs):
    for j, blocks in enumerate(by_sender(refs[:5])[offset] for offset in OFFSETS):
        for u, block in zip(OFFSETS, blocks):
            place_on_line(refs[5:], u, j, block)


def regroup(got):
    depth, chip_rows = got[0].shape[1:]
    return pl.pallas_call(
        regroup_kernel,
        out_shape=line_shapes(depth, chip_rows, got[0].dtype),
        in_specs=[VMEM] * 5,
        out_specs=(VMEM,) * 3,
        compiler_params=pltpu.CompilerParams(vmem_limit_bytes=8 << 20),
        name="regroup",
    )(*got)


def collect_kernel(*refs):
    for j, blocks in enumerate(by_sender(refs[:5])[offset] for offset in OFFSETS):
        for i, block in enumerate(blocks):
            refs[5][j * SIDE + i] = block


def collect(got):
    depth, chip_rows = got[0].shape[1:]
    return pl.pallas_call(
        collect_kernel,
        out_shape=jax.ShapeDtypeStruct((PLANE, depth, chip_rows), got[0].dtype),
        in_specs=[VMEM] * 5,
        out_specs=VMEM,
        compiler_params=pltpu.CompilerParams(vmem_limit_bytes=8 << 20),
        name="collect",
    )(*got)


def along_line(blocks, order):
    kept, back, ahead = blocks
    from_ahead, from_behind = along_plane(back, order, -1), along_plane(ahead, order, 1)
    far_behind = along_plane(from_behind[SIDE:], order, 1)
    far_ahead = along_plane(from_ahead[SIDE:], order, -1)
    return kept, from_ahead, from_behind, far_behind, far_ahead


def pair_kernel(*refs):
    mine_refs, got_ref, out_refs = refs[:SIDE], refs[SIDE], refs[SIDE + 1 :]
    depth = got_ref.shape[1]
    for dy in range(SIDE):
        out_refs[dy][:depth, :] = mine_refs[dy][...]
        out_refs[dy][depth:, :] = got_ref[dy]


def pair(mine, got):
    window = jax.ShapeDtypeStruct((CORES * got.shape[1], WIDE), got.dtype)
    return pl.pallas_call(
        pair_kernel,
        out_shape=(window,) * SIDE,
        in_specs=[VMEM] * (SIDE + 1),
        out_specs=(VMEM,) * SIDE,
        compiler_params=pltpu.CompilerParams(vmem_limit_bytes=6 << 20),
        name="pair",
    )(*mine, got)


OFFSETS = (0, -1, 1, 2)
OWN = tuple((dcore, 0) for dcore in range(CORES))
OTHERS = tuple((dcore, dy) for dy in range(1, SIDE) for dcore in range(CORES))


def at(v, *us):
    return tuple((u, v) for u in us)


def gathered_briefly(own):
    before, after = along_plane(own, 0, 1), along_plane(own, 0, -1)
    far = along_plane(before, 0, 1)
    line = join([own, before, after, far])
    left, right = along_plane(line, 1, 1), along_plane(line, 1, -1)
    cut = line.shape[0] // 2
    opposite = along_plane(left[:cut], 1, 1), along_plane(right[cut:], 1, -1)
    first = sum((at(v, 0, -1, 1, 2) for v in (0, -1, 1)), ())
    last = join(opposite)
    return (first, join([line, left, right])), (at(2, 0, -1, 1, 2), last)


def gathered(own):
    cut = own.shape[0] // 2
    before, after = along_plane(own, 0, 1), along_plane(own, 0, -1)
    near = join([before, after])
    far = along_plane(before, 0, 1)
    near_sides = along_plane(near, 1, 1), along_plane(near, 1, -1)
    own_sides = along_plane(own, 1, 1), along_plane(own, 1, -1)
    far_sides = along_plane(far, 1, 1), along_plane(far, 1, -1)
    own_opposite = along_plane(own_sides[0], 1, 1)
    near_opposite = along_plane(near_sides[0][:cut], 1, 1), along_plane(near_sides[1][cut:], 1, -1)
    far_opposite = along_plane(far_sides[1], 1, -1)

    first = at(0, 0, -1, 1, 2) + at(-1, 0) + at(1, 0)
    parts = [(first, 0, join([own, near, far, *own_sides]))]
    parts += [(at(v, -1, 1), 0, block) for v, block in zip((-1, 1), near_sides)]
    parts += [(at(-1, 2) + at(1, 2) + at(2, 0), 0, join([*far_sides, own_opposite]))]
    parts += [(at(2, -1, 1), 0, near_opposite[0]), (at(2, -1, 1), len(OTHERS) // 2, near_opposite[1])]
    parts += [(at(2, 2), 0, far_opposite)]
    return parts


def arrange_kernel(layout, *refs):
    in_refs, out_refs = refs[: -len(layout)], refs[-len(layout) :]
    depth = in_refs[0].shape[1]
    for blocks, out_ref in zip(layout, out_refs):
        for i, (u, v, dcore, place) in enumerate(blocks):
            first, second = (u, v) if dcore == 0 else (v, u)
            chip = OFFSETS.index(second) * SIDE + OFFSETS.index(first)
            out_ref[i * depth : (i + 1) * depth, :] = in_refs[dcore][place * PLANE + chip]


def arrange(layout, *rows):
    depth, chip_rows = rows[0].shape[1:]
    size = sum(map(len, layout)) * depth * chip_rows * rows[0].dtype.itemsize
    return pl.pallas_call(
        lambda *refs: arrange_kernel(layout, *refs),
        out_shape=tuple(jax.ShapeDtypeStruct((len(blocks) * depth, chip_rows), rows[0].dtype) for blocks in layout),
        in_specs=[VMEM] * CORES,
        out_specs=(VMEM,) * len(layout),
        compiler_params=pltpu.CompilerParams(vmem_limit_bytes=2 * size + (1 << 20)),
        cost_estimate=pl.CostEstimate(flops=0, bytes_accessed=2 * size, transcendentals=0),
        name="arrange",
    )(*rows)


def halve_kernel(tile_ref, kept_ref, sent_ref):
    rows = kept_ref.shape[0]
    for core in range(CORES):

        @pl.when(lax.axis_index("core") == core)
        def _():
            kept_ref[...] = tile_ref[core * rows : (core + 1) * rows, :]
            sent_ref[...] = tile_ref[(1 - core) * rows : (2 - core) * rows, :]


def halve(tile):
    half = jax.ShapeDtypeStruct((tile.shape[0] // CORES, tile.shape[1]), tile.dtype)
    return pl.pallas_call(
        halve_kernel,
        out_shape=(half, half),
        in_specs=[VMEM],
        out_specs=(VMEM, VMEM),
        compiler_params=pltpu.CompilerParams(vmem_limit_bytes=8 << 20),
        name="halve",
    )(tile)


def assemble_kernel(kept_ref, got_ref, out_ref):
    rest = out_ref.shape[1] - WIDE
    for core in range(CORES):

        @pl.when(lax.axis_index("core") == core)
        def _():
            first, last = (kept_ref, got_ref) if core == 0 else (got_ref, kept_ref)
            out_ref[:, :WIDE] = first[...]
            out_ref[:, WIDE:] = last[:, :rest]


def assemble(kept, got, columns):
    return pl.pallas_call(
        assemble_kernel,
        out_shape=jax.ShapeDtypeStruct((got.shape[0], columns), got.dtype),
        in_specs=[VMEM, VMEM],
        out_specs=VMEM,
        compiler_params=pltpu.CompilerParams(vmem_limit_bytes=8 << 20),
        name="assemble",
    )(kept, got)


def body(b_tensor, aux_counts):
    basis = b_tensor.shape[0]
    mine, theirs, rows = pack(aux_counts, b_tensor.transpose(1, 2, 0))

    got = swap_cores(theirs)
    windows = pair(mine, got)
    others = join([along_y(windows[-dy % SIDE], -dy % SIDE) for dy in range(1, SIDE)])
    rows = along_line(rows, 0)
    rows = regroup(rows)
    rows = along_line(rows, 1)
    rows = collect(rows)
    early = gathered_briefly(windows[0])
    parts = gathered(others)

    left, right = along_y(rows, 1), along_y(rows, -1)
    half = PLANE // 2
    far = along_y(left[:half], 1), along_y(right[half:], -1)
    rest = join([right, *far, left])
    other_rows = swap_cores(rows)
    other_rest = swap_cores(rest)

    def product(weight, block):
        return lax.dot_general(weight, block, (((0,), (0,)), ((), ())), preferred_element_type=jnp.float32)

    layout = [[(u, v, dcore, dy) for u, v in offsets for dcore, dy in OWN] for offsets, _ in early]
    weights = arrange(layout, rows, other_rows)
    tile = product(weights[0], early[0][1])
    layout = []
    for offsets, skipped, block in parts:
        blocks = [(u, v, dcore, dy - 1) for u, v in offsets for dcore, dy in OTHERS]
        layout.append(blocks[skipped : skipped + block.shape[0] // rows.shape[1]])
    weights = (*arrange(layout, rest, other_rest), weights[1])
    blocks = [block for *_, block in parts] + [early[1][1]]
    for i in (1, 2, len(parts), 0, 4, 5, 3, *range(6, len(parts))):
        tile = lax.optimization_barrier(tile + product(weights[i], blocks[i]))

    kept, sent = halve(tile)
    return assemble(kept, swap_cores(sent), basis // SIDE)


def solution(mesh):
    fine = Mesh(mesh.devices.reshape(SIDE, SIDE, SIDE, CORES), ("y", "x", "z", "core"))
    return jax.shard_map(
        body,
        mesh=fine,
        in_specs=(P(None, "y", ("x", "z", "core")), P()),
        out_specs=P(("x", "z", "core"), "y"),
        check_vma=False,
    )
```

```python
import jax
import jax.numpy as jnp
from jax import lax
from jax.experimental import pallas as pl
from jax.experimental.pallas import tpu as pltpu
from jax.sharding import Mesh, PartitionSpec as P


SIDE = 4
CORES = 2
PLANE = SIDE * SIDE
WIDE = 1280
VMEM = pl.BlockSpec(memory_space=pltpu.VMEM)
SMEM = pl.BlockSpec(memory_space=pltpu.SMEM)


def along_y(block, step):
    return lax.ppermute(block, "y", [(i, (i + step) % SIDE) for i in range(SIDE)])


def swap_cores(block):
    return lax.ppermute(block, "core", [(0, 1), (1, 0)])


def along_plane(block, order, step):
    route = []
    for x in range(SIDE):
        for z in range(SIDE):
            for core in range(CORES):
                to = ((x + step) % SIDE, z) if core == order else (x, (z + step) % SIDE)
                route.append(((x * SIDE + z) * CORES + core, (to[0] * SIDE + to[1]) * CORES + core))
    return lax.ppermute(block, ("x", "z", "core"), route)


def join(blocks):
    def kernel(*refs):
        at = 0
        for ref in refs[:-1]:
            refs[-1][at : at + ref.shape[0]] = ref[...]
            at += ref.shape[0]

    total = sum(block.shape[0] for block in blocks)
    joined = jax.ShapeDtypeStruct((total, *blocks[0].shape[1:]), blocks[0].dtype)
    size = joined.size * joined.dtype.itemsize
    return pl.pallas_call(
        kernel,
        out_shape=joined,
        in_specs=[VMEM] * len(blocks),
        out_specs=VMEM,
        compiler_params=pltpu.CompilerParams(vmem_limit_bytes=2 * size + (1 << 18)),
        cost_estimate=pl.CostEstimate(flops=0, bytes_accessed=2 * size, transcendentals=0),
        name="join",
    )(*blocks)


def pack_kernel(count_ref, terms_ref, *refs):
    mine_refs, theirs_ref, rows_refs, (windows, rows) = refs[:SIDE], refs[SIDE], refs[SIDE + 1 : -2], refs[-2:]
    slots, orbitals, basis = terms_ref.shape
    columns = basis // SIDE
    chip_rows = rows.shape[2]
    x, y, z, core = (lax.axis_index(name) for name in ("x", "y", "z", "core"))
    for s in range(slots):
        live = s < count_ref[y]
        at = pl.ds(s * orbitals, orbitals)
        for p in range(SIDE):
            for q in range(CORES):
                start = p * columns + q * WIDE
                width = min(WIDE, basis - start)
                block = terms_ref[s, :, start : start + width]
                windows[p * CORES + q, at, :width] = jnp.where(live, block, jnp.zeros_like(block))
                if width < WIDE:
                    windows[p * CORES + q, at, width:] = jnp.zeros((orbitals, WIDE - width), block.dtype)
        for i in range(PLANE):
            block = terms_ref[s, :, i * chip_rows : (i + 1) * chip_rows]
            rows[i, at, :] = jnp.where(live, block, jnp.zeros_like(block))
    for dy in range(SIDE):
        plane = lax.rem(y + dy, SIDE) * CORES
        mine_refs[dy][...] = windows[plane + core]
        theirs_ref[dy] = windows[plane + 1 - core]
    for u, rows_ref in zip(OFFSETS, rows_refs):
        for i, v in enumerate(OFFSETS):
            dx, dz = jnp.where(core == 0, u, v), jnp.where(core == 0, v, u)
            rows_ref[i] = rows[lax.rem(x + dx + SIDE, SIDE) * SIDE + lax.rem(z + dz + SIDE, SIDE)]


def pack(counts, terms):
    slots, orbitals, basis = terms.shape
    depth = slots * orbitals
    window = jax.ShapeDtypeStruct((depth, WIDE), terms.dtype)
    other_windows = jax.ShapeDtypeStruct((SIDE, depth, WIDE), terms.dtype)
    line_rows = jax.ShapeDtypeStruct((SIDE, depth, basis // PLANE), terms.dtype)
    *mine, theirs, rows_0, rows_1, rows_2, rows_3 = pl.pallas_call(
        pack_kernel,
        out_shape=(window,) * SIDE + (other_windows,) + (line_rows,) * SIDE,
        in_specs=[SMEM, VMEM],
        out_specs=(VMEM,) * (2 * SIDE + 1),
        scratch_shapes=[
            pltpu.VMEM((CORES * SIDE, depth, WIDE), terms.dtype),
            pltpu.VMEM((PLANE, depth, basis // PLANE), terms.dtype),
        ],
        compiler_params=pltpu.CompilerParams(vmem_limit_bytes=12 << 20),
        name="pack",
    )(counts, terms)
    return mine, theirs, (rows_0, rows_1, rows_2, rows_3)


def regroup_kernel(*refs):
    for i, in_ref in enumerate(refs[:SIDE]):
        for j, out_ref in enumerate(refs[SIDE:]):
            out_ref[i] = in_ref[j]


def regroup(blocks):
    return pl.pallas_call(
        regroup_kernel,
        out_shape=tuple(jax.ShapeDtypeStruct(block.shape, block.dtype) for block in blocks),
        in_specs=[VMEM] * SIDE,
        out_specs=(VMEM,) * SIDE,
        compiler_params=pltpu.CompilerParams(vmem_limit_bytes=6 << 20),
        name="regroup",
    )(*blocks)


def along_line(blocks, order):
    got = {0: blocks[0]}
    for offset, block in zip(OFFSETS[1:], blocks[1:]):
        got[-offset if offset < 2 else 2] = along_plane(block, order, offset)
    return [got[offset] for offset in OFFSETS]


def pair_kernel(*refs):
    mine_refs, got_ref, out_refs = refs[:SIDE], refs[SIDE], refs[SIDE + 1 :]
    depth = got_ref.shape[1]
    for dy in range(SIDE):
        out_refs[dy][:depth, :] = mine_refs[dy][...]
        out_refs[dy][depth:, :] = got_ref[dy]


def pair(mine, got):
    window = jax.ShapeDtypeStruct((CORES * got.shape[1], WIDE), got.dtype)
    return pl.pallas_call(
        pair_kernel,
        out_shape=(window,) * SIDE,
        in_specs=[VMEM] * (SIDE + 1),
        out_specs=(VMEM,) * SIDE,
        compiler_params=pltpu.CompilerParams(vmem_limit_bytes=6 << 20),
        name="pair",
    )(*mine, got)


OFFSETS = (0, -1, 1, 2)
OWN = tuple((dcore, 0) for dcore in range(CORES))
OTHERS = tuple((dcore, dy) for dy in range(1, SIDE) for dcore in range(CORES))


def at(sources, v, *us):
    return tuple((u, v, *source) for u in us for source in sources)


def gathered(early, late):
    early_before, early_after = along_plane(early, 0, 1), along_plane(early, 0, -1)
    line = join([early, early_before, early_after])
    left, right = along_plane(line, 1, 1), along_plane(line, 1, -1)
    cut = line.shape[0] // 2
    opposite = along_plane(left[:cut], 1, 1), along_plane(right[cut:], 1, -1)

    before, after = along_plane(late, 0, 1), along_plane(late, 0, -1)
    near = join([before, after])
    both_before = join([early_before, before])
    far = along_plane(both_before, 0, 1)
    near_sides = along_plane(near, 1, 1), along_plane(near, 1, -1)
    own_sides = along_plane(late, 1, 1), along_plane(late, 1, -1)
    far_sides = along_plane(far, 1, 1), along_plane(far, 1, -1)
    own_opposite = along_plane(own_sides[0], 1, 1)
    cut = late.shape[0] // 2
    near_opposite = along_plane(near_sides[0][:cut], 1, 1), along_plane(near_sides[1][cut:], 1, -1)
    far_opposite = along_plane(far_sides[1], 1, -1)

    early_opposite = join(opposite)
    first = join([late, near, far, *own_sides])
    middle = join([*far_sides, own_opposite])
    ends = at(OTHERS, 2, -1, 1)
    return (
        (sum((at(OWN, v, 0, -1, 1) for v in (0, -1, 1)), ()), join([line, left, right])),
        (at(OWN, 2, 0, -1, 1), early_opposite),
        (at(OTHERS, 0, 0, -1, 1) + at(OWN + OTHERS, 0, 2) + at(OTHERS, -1, 0) + at(OTHERS, 1, 0), first),
        (at(OTHERS, -1, -1, 1), near_sides[0]),
        (at(OTHERS, 1, -1, 1), near_sides[1]),
        (at(OWN + OTHERS, -1, 2) + at(OWN + OTHERS, 1, 2) + at(OTHERS, 2, 0), middle),
        (ends[: len(ends) // 4], near_opposite[0]),
        (ends[len(ends) // 4 :], near_opposite[1]),
        (at(OWN + OTHERS, 2, 2), far_opposite),
    )


def arrange_kernel(layout, *refs):
    in_refs, out_refs = refs[: -len(layout)], refs[-len(layout) :]
    depth = in_refs[0].shape[1]
    for blocks, out_ref in zip(layout, out_refs):
        for i, (u, v, dcore, dy) in enumerate(blocks):
            first, second = (u, v) if dcore == 0 else (v, u)
            chip = OFFSETS.index(second) * SIDE + OFFSETS.index(first)
            source = in_refs[dcore][chip] if dy == 0 else in_refs[CORES + dcore][(dy - 1) * PLANE + chip]
            out_ref[i * depth : (i + 1) * depth, :] = source


def arrange(layout, *rows):
    depth, chip_rows = rows[0].shape[1:]
    size = sum(map(len, layout)) * depth * chip_rows * rows[0].dtype.itemsize
    return pl.pallas_call(
        lambda *refs: arrange_kernel(layout, *refs),
        out_shape=tuple(jax.ShapeDtypeStruct((len(blocks) * depth, chip_rows), rows[0].dtype) for blocks in layout),
        in_specs=[VMEM] * len(rows),
        out_specs=(VMEM,) * len(layout),
        compiler_params=pltpu.CompilerParams(vmem_limit_bytes=2 * size + (1 << 20)),
        cost_estimate=pl.CostEstimate(flops=0, bytes_accessed=2 * size, transcendentals=0),
        name="arrange",
    )(*rows)


def halve_kernel(tile_ref, kept_ref, sent_ref):
    rows = kept_ref.shape[0]
    for core in range(CORES):

        @pl.when(lax.axis_index("core") == core)
        def _():
            kept_ref[...] = tile_ref[core * rows : (core + 1) * rows, :]
            sent_ref[...] = tile_ref[(1 - core) * rows : (2 - core) * rows, :]


def halve(tile):
    half = jax.ShapeDtypeStruct((tile.shape[0] // CORES, tile.shape[1]), tile.dtype)
    return pl.pallas_call(
        halve_kernel,
        out_shape=(half, half),
        in_specs=[VMEM],
        out_specs=(VMEM, VMEM),
        compiler_params=pltpu.CompilerParams(vmem_limit_bytes=8 << 20),
        name="halve",
    )(tile)


def assemble_kernel(kept_ref, got_ref, out_ref):
    rest = out_ref.shape[1] - WIDE
    for core in range(CORES):

        @pl.when(lax.axis_index("core") == core)
        def _():
            first, last = (kept_ref, got_ref) if core == 0 else (got_ref, kept_ref)
            out_ref[:, :WIDE] = first[...]
            out_ref[:, WIDE:] = last[:, :rest]


def assemble(kept, got, columns):
    return pl.pallas_call(
        assemble_kernel,
        out_shape=jax.ShapeDtypeStruct((got.shape[0], columns), got.dtype),
        in_specs=[VMEM, VMEM],
        out_specs=VMEM,
        compiler_params=pltpu.CompilerParams(vmem_limit_bytes=8 << 20),
        name="assemble",
    )(kept, got)


def body(b_tensor, aux_counts):
    basis = b_tensor.shape[0]
    mine, theirs, rows = pack(aux_counts, b_tensor.transpose(1, 2, 0))

    got = swap_cores(theirs)
    windows = pair(mine, got)
    others = join([along_y(windows[-dy % SIDE], -dy % SIDE) for dy in range(1, SIDE)])
    rows = along_line(rows, 0)
    rows = regroup(rows)
    rows = along_line(rows, 1)
    rows = join(rows)
    parts = gathered(windows[0], others)

    left, right = along_y(rows, 1), along_y(rows, -1)
    half = PLANE // 2
    far = along_y(left[:half], 1), along_y(right[half:], -1)
    rest = join([right, *far, left])
    other_rows = swap_cores(rows)
    other_rest = swap_cores(rest)

    def product(weight, block):
        return lax.dot_general(weight, block, (((0,), (0,)), ((), ())), preferred_element_type=jnp.float32)

    weights = arrange([terms for terms, _ in parts[:2]], rows, other_rows)
    weights += arrange([terms for terms, _ in parts[2:]], rows, other_rows, rest, other_rest)
    tile = product(weights[0], parts[0][1])
    for i in (3, 4, 1, 2, 6, 7, 5, 8):
        tile = lax.optimization_barrier(tile + product(weights[i], parts[i][1]))

    kept, sent = halve(tile)
    return assemble(kept, swap_cores(sent), basis // SIDE)


def solution(mesh):
    fine = Mesh(mesh.devices.reshape(SIDE, SIDE, SIDE, CORES), ("y", "x", "z", "core"))
    return jax.shard_map(
        body,
        mesh=fine,
        in_specs=(P(None, "y", ("x", "z", "core")), P()),
        out_specs=P(("x", "z", "core"), "y"),
        check_vma=False,
    )
```

```python
import jax
import jax.numpy as jnp
from jax import lax
from jax.experimental import pallas as pl
from jax.experimental.pallas import tpu as pltpu
from jax.sharding import Mesh, PartitionSpec as P


SIDE = 4
CORES = 2
PLANE = SIDE * SIDE
WIDE = 1280
VMEM = pl.BlockSpec(memory_space=pltpu.VMEM)
SMEM = pl.BlockSpec(memory_space=pltpu.SMEM)


def along_y(block, step):
    return lax.ppermute(block, "y", [(i, (i + step) % SIDE) for i in range(SIDE)])


def swap_cores(block):
    return lax.ppermute(block, "core", [(0, 1), (1, 0)])


def along_plane(block, order, step):
    route = []
    for x in range(SIDE):
        for z in range(SIDE):
            for core in range(CORES):
                to = ((x + step) % SIDE, z) if core == order else (x, (z + step) % SIDE)
                route.append(((x * SIDE + z) * CORES + core, (to[0] * SIDE + to[1]) * CORES + core))
    return lax.ppermute(block, ("x", "z", "core"), route)


def join(blocks):
    def kernel(*refs):
        at = 0
        for ref in refs[:-1]:
            refs[-1][at : at + ref.shape[0]] = ref[...]
            at += ref.shape[0]

    total = sum(block.shape[0] for block in blocks)
    joined = jax.ShapeDtypeStruct((total, *blocks[0].shape[1:]), blocks[0].dtype)
    size = joined.size * joined.dtype.itemsize
    return pl.pallas_call(
        kernel,
        out_shape=joined,
        in_specs=[VMEM] * len(blocks),
        out_specs=VMEM,
        compiler_params=pltpu.CompilerParams(vmem_limit_bytes=2 * size + (1 << 18)),
        cost_estimate=pl.CostEstimate(flops=0, bytes_accessed=2 * size, transcendentals=0),
        name="join",
    )(*blocks)


def pack_kernel(count_ref, terms_ref, *refs):
    mine_refs, theirs_ref, rows_refs, (windows, rows) = refs[:SIDE], refs[SIDE], refs[SIDE + 1 : -2], refs[-2:]
    slots, orbitals, basis = terms_ref.shape
    columns = basis // SIDE
    chip_rows = rows.shape[2]
    x, y, z, core = (lax.axis_index(name) for name in ("x", "y", "z", "core"))
    for s in range(slots):
        live = s < count_ref[y]
        at = pl.ds(s * orbitals, orbitals)
        for p in range(SIDE):
            for q in range(CORES):
                start = p * columns + q * WIDE
                width = min(WIDE, basis - start)
                block = terms_ref[s, :, start : start + width]
                windows[p * CORES + q, at, :width] = jnp.where(live, block, jnp.zeros_like(block))
                if width < WIDE:
                    windows[p * CORES + q, at, width:] = jnp.zeros((orbitals, WIDE - width), block.dtype)
        for i in range(PLANE):
            block = terms_ref[s, :, i * chip_rows : (i + 1) * chip_rows]
            rows[i, at, :] = jnp.where(live, block, jnp.zeros_like(block))
    for dy in range(SIDE):
        plane = lax.rem(y + dy, SIDE) * CORES
        mine_refs[dy][...] = windows[plane + core]
        theirs_ref[dy] = windows[plane + 1 - core]
    for u, rows_ref in zip(OFFSETS, rows_refs):
        for i, v in enumerate(OFFSETS):
            dx, dz = jnp.where(core == 0, u, v), jnp.where(core == 0, v, u)
            rows_ref[i] = rows[lax.rem(x + dx + SIDE, SIDE) * SIDE + lax.rem(z + dz + SIDE, SIDE)]


def pack(counts, terms):
    slots, orbitals, basis = terms.shape
    depth = slots * orbitals
    window = jax.ShapeDtypeStruct((depth, WIDE), terms.dtype)
    other_windows = jax.ShapeDtypeStruct((SIDE, depth, WIDE), terms.dtype)
    line_rows = jax.ShapeDtypeStruct((SIDE, depth, basis // PLANE), terms.dtype)
    *mine, theirs, rows_0, rows_1, rows_2, rows_3 = pl.pallas_call(
        pack_kernel,
        out_shape=(window,) * SIDE + (other_windows,) + (line_rows,) * SIDE,
        in_specs=[SMEM, VMEM],
        out_specs=(VMEM,) * (2 * SIDE + 1),
        scratch_shapes=[
            pltpu.VMEM((CORES * SIDE, depth, WIDE), terms.dtype),
            pltpu.VMEM((PLANE, depth, basis // PLANE), terms.dtype),
        ],
        compiler_params=pltpu.CompilerParams(vmem_limit_bytes=12 << 20),
        name="pack",
    )(counts, terms)
    return mine, theirs, (rows_0, rows_1, rows_2, rows_3)


def regroup_kernel(*refs):
    for i, in_ref in enumerate(refs[:SIDE]):
        for j, out_ref in enumerate(refs[SIDE:]):
            out_ref[i] = in_ref[j]


def regroup(blocks):
    return pl.pallas_call(
        regroup_kernel,
        out_shape=tuple(jax.ShapeDtypeStruct(block.shape, block.dtype) for block in blocks),
        in_specs=[VMEM] * SIDE,
        out_specs=(VMEM,) * SIDE,
        compiler_params=pltpu.CompilerParams(vmem_limit_bytes=6 << 20),
        name="regroup",
    )(*blocks)


def along_line(blocks, order):
    got = {0: blocks[0]}
    for offset, block in zip(OFFSETS[1:], blocks[1:]):
        got[-offset if offset < 2 else 2] = along_plane(block, order, offset)
    return [got[offset] for offset in OFFSETS]


def pair_kernel(*refs):
    mine_refs, got_ref, out_refs = refs[:SIDE], refs[SIDE], refs[SIDE + 1 :]
    depth = got_ref.shape[1]
    for dy in range(SIDE):
        out_refs[dy][:depth, :] = mine_refs[dy][...]
        out_refs[dy][depth:, :] = got_ref[dy]


def pair(mine, got):
    window = jax.ShapeDtypeStruct((CORES * got.shape[1], WIDE), got.dtype)
    return pl.pallas_call(
        pair_kernel,
        out_shape=(window,) * SIDE,
        in_specs=[VMEM] * (SIDE + 1),
        out_specs=(VMEM,) * SIDE,
        compiler_params=pltpu.CompilerParams(vmem_limit_bytes=6 << 20),
        name="pair",
    )(*mine, got)


OFFSETS = (0, -1, 1, 2)
OWN = tuple((dcore, 0) for dcore in range(CORES))
OTHERS = tuple((dcore, dy) for dy in range(1, SIDE) for dcore in range(CORES))


def at(sources, v, *us):
    return tuple((u, v, *source) for u in us for source in sources)


def gathered(early, late):
    early_before, early_after = along_plane(early, 0, 1), along_plane(early, 0, -1)
    line = join([early, early_before, early_after])
    left, right = along_plane(line, 1, 1), along_plane(line, 1, -1)
    cut = line.shape[0] // 2
    opposite = along_plane(left[:cut], 1, 1), along_plane(right[cut:], 1, -1)

    before, after = along_plane(late, 0, 1), along_plane(late, 0, -1)
    near = join([before, after])
    both_before = join([early_before, before])
    far = along_plane(both_before, 0, 1)
    near_right = along_plane(near, 1, -1)
    far_sides = along_plane(far, 1, 1), along_plane(far, 1, -1)
    near_left = along_plane(near, 1, 1)
    own_sides = along_plane(late, 1, 1), along_plane(late, 1, -1)
    cut = late.shape[0] // 2
    opposite_right = along_plane(near_right[cut:], 1, -1)
    far_opposite = along_plane(far_sides[1], 1, -1)
    opposite_left = along_plane(near_left[:cut], 1, 1)
    own_opposite = along_plane(own_sides[0], 1, 1)

    early_opposite = join(opposite)
    first = join([late, near, far, *own_sides])
    end = join([opposite_left, own_opposite])
    ends = at(OTHERS, 2, -1, 1)
    cut = len(ends) // 4
    return (
        (sum((at(OWN, v, 0, -1, 1) for v in (0, -1, 1)), ()), join([line, left, right])),
        (at(OWN, 2, 0, -1, 1), early_opposite),
        (at(OTHERS, 0, 0, -1, 1) + at(OWN + OTHERS, 0, 2) + at(OTHERS, -1, 0) + at(OTHERS, 1, 0), first),
        (at(OTHERS, -1, -1, 1), near_left),
        (at(OTHERS, 1, -1, 1), near_right),
        (at(OWN + OTHERS, -1, 2) + at(OWN + OTHERS, 1, 2), join(far_sides)),
        (ends[:cut] + at(OTHERS, 2, 0), end),
        (ends[cut:], opposite_right),
        (at(OWN + OTHERS, 2, 2), far_opposite),
    )


def arrange_kernel(layout, *refs):
    in_refs, out_refs = refs[: -len(layout)], refs[-len(layout) :]
    depth = in_refs[0].shape[1]
    for blocks, out_ref in zip(layout, out_refs):
        for i, (u, v, dcore, dy) in enumerate(blocks):
            first, second = (u, v) if dcore == 0 else (v, u)
            chip = OFFSETS.index(second) * SIDE + OFFSETS.index(first)
            source = in_refs[dcore][chip] if dy == 0 else in_refs[CORES + dcore][(dy - 1) * PLANE + chip]
            out_ref[i * depth : (i + 1) * depth, :] = source


def arrange(layout, *rows):
    depth, chip_rows = rows[0].shape[1:]
    size = sum(map(len, layout)) * depth * chip_rows * rows[0].dtype.itemsize
    return pl.pallas_call(
        lambda *refs: arrange_kernel(layout, *refs),
        out_shape=tuple(jax.ShapeDtypeStruct((len(blocks) * depth, chip_rows), rows[0].dtype) for blocks in layout),
        in_specs=[VMEM] * len(rows),
        out_specs=(VMEM,) * len(layout),
        compiler_params=pltpu.CompilerParams(vmem_limit_bytes=2 * size + (1 << 20)),
        cost_estimate=pl.CostEstimate(flops=0, bytes_accessed=2 * size, transcendentals=0),
        name="arrange",
    )(*rows)


def halve_kernel(tile_ref, kept_ref, sent_ref):
    rows = kept_ref.shape[0]
    for core in range(CORES):

        @pl.when(lax.axis_index("core") == core)
        def _():
            kept_ref[...] = tile_ref[core * rows : (core + 1) * rows, :]
            sent_ref[...] = tile_ref[(1 - core) * rows : (2 - core) * rows, :]


def halve(tile):
    half = jax.ShapeDtypeStruct((tile.shape[0] // CORES, tile.shape[1]), tile.dtype)
    return pl.pallas_call(
        halve_kernel,
        out_shape=(half, half),
        in_specs=[VMEM],
        out_specs=(VMEM, VMEM),
        compiler_params=pltpu.CompilerParams(vmem_limit_bytes=8 << 20),
        name="halve",
    )(tile)


def assemble_kernel(kept_ref, got_ref, out_ref):
    rest = out_ref.shape[1] - WIDE
    for core in range(CORES):

        @pl.when(lax.axis_index("core") == core)
        def _():
            first, last = (kept_ref, got_ref) if core == 0 else (got_ref, kept_ref)
            out_ref[:, :WIDE] = first[...]
            out_ref[:, WIDE:] = last[:, :rest]


def assemble(kept, got, columns):
    return pl.pallas_call(
        assemble_kernel,
        out_shape=jax.ShapeDtypeStruct((got.shape[0], columns), got.dtype),
        in_specs=[VMEM, VMEM],
        out_specs=VMEM,
        compiler_params=pltpu.CompilerParams(vmem_limit_bytes=8 << 20),
        name="assemble",
    )(kept, got)


def body(b_tensor, aux_counts):
    basis = b_tensor.shape[0]
    mine, theirs, rows = pack(aux_counts, b_tensor.transpose(1, 2, 0))

    got = swap_cores(theirs)
    windows = pair(mine, got)
    others = join([along_y(windows[-dy % SIDE], -dy % SIDE) for dy in range(1, SIDE)])
    rows = along_line(rows, 0)
    rows = regroup(rows)
    rows = along_line(rows, 1)
    rows = join(rows)
    parts = gathered(windows[0], others)

    left, right = along_y(rows, 1), along_y(rows, -1)
    half = PLANE // 2
    far = along_y(left[:half], 1), along_y(right[half:], -1)
    rest = join([right, *far, left])
    other_rows = swap_cores(rows)
    other_rest = swap_cores(rest)

    def product(weight, block):
        return lax.dot_general(weight, block, (((0,), (0,)), ((), ())), preferred_element_type=jnp.float32)

    weights = arrange([terms for terms, _ in parts[:2]], rows, other_rows)
    weights += arrange([terms for terms, _ in parts[2:]], rows, other_rows, rest, other_rest)
    tile = product(weights[0], parts[0][1])
    for i in (4, 1, 5, 3, 2, 7, 6, 8):
        tile = lax.optimization_barrier(tile + product(weights[i], parts[i][1]))

    kept, sent = halve(tile)
    return assemble(kept, swap_cores(sent), basis // SIDE)


def solution(mesh):
    fine = Mesh(mesh.devices.reshape(SIDE, SIDE, SIDE, CORES), ("y", "x", "z", "core"))
    return jax.shard_map(
        body,
        mesh=fine,
        in_specs=(P(None, "y", ("x", "z", "core")), P()),
        out_specs=P(("x", "z", "core"), "y"),
        check_vma=False,
    )
```

```python
import jax
import jax.numpy as jnp
from jax import lax
from jax.experimental import pallas as pl
from jax.experimental.pallas import tpu as pltpu
from jax.sharding import Mesh, PartitionSpec as P


SIDE = 4
CORES = 2
PLANE = SIDE * SIDE
WIDE = 1280
VMEM = pl.BlockSpec(memory_space=pltpu.VMEM)
SMEM = pl.BlockSpec(memory_space=pltpu.SMEM)


def along_y(block, step):
    return lax.ppermute(block, "y", [(i, (i + step) % SIDE) for i in range(SIDE)])


def swap_cores(block):
    return lax.ppermute(block, "core", [(0, 1), (1, 0)])


def along_plane(block, order, step):
    route = []
    for x in range(SIDE):
        for z in range(SIDE):
            for core in range(CORES):
                to = ((x + step) % SIDE, z) if core == order else (x, (z + step) % SIDE)
                route.append(((x * SIDE + z) * CORES + core, (to[0] * SIDE + to[1]) * CORES + core))
    return lax.ppermute(block, ("x", "z", "core"), route)


def join(blocks):
    def kernel(*refs):
        at = 0
        for ref in refs[:-1]:
            refs[-1][at : at + ref.shape[0]] = ref[...]
            at += ref.shape[0]

    total = sum(block.shape[0] for block in blocks)
    joined = jax.ShapeDtypeStruct((total, *blocks[0].shape[1:]), blocks[0].dtype)
    size = joined.size * joined.dtype.itemsize
    return pl.pallas_call(
        kernel,
        out_shape=joined,
        in_specs=[VMEM] * len(blocks),
        out_specs=VMEM,
        compiler_params=pltpu.CompilerParams(vmem_limit_bytes=2 * size + (1 << 18)),
        cost_estimate=pl.CostEstimate(flops=0, bytes_accessed=2 * size, transcendentals=0),
        name="join",
    )(*blocks)


def pack_kernel(count_ref, terms_ref, *refs):
    mine_refs, theirs_ref, rows_refs, (windows, rows) = refs[:SIDE], refs[SIDE], refs[SIDE + 1 : -2], refs[-2:]
    slots, orbitals, basis = terms_ref.shape
    columns = basis // SIDE
    chip_rows = rows.shape[2]
    x, y, z, core = (lax.axis_index(name) for name in ("x", "y", "z", "core"))
    for s in range(slots):
        live = s < count_ref[y]
        at = pl.ds(s * orbitals, orbitals)
        for p in range(SIDE):
            for q in range(CORES):
                start = p * columns + q * WIDE
                width = min(WIDE, basis - start)
                block = terms_ref[s, :, start : start + width]
                windows[p * CORES + q, at, :width] = jnp.where(live, block, jnp.zeros_like(block))
                if width < WIDE:
                    windows[p * CORES + q, at, width:] = jnp.zeros((orbitals, WIDE - width), block.dtype)
        for i in range(PLANE):
            block = terms_ref[s, :, i * chip_rows : (i + 1) * chip_rows]
            rows[i, at, :] = jnp.where(live, block, jnp.zeros_like(block))
    for dy in range(SIDE):
        plane = lax.rem(y + dy, SIDE) * CORES
        mine_refs[dy][...] = windows[plane + core]
        theirs_ref[dy] = windows[plane + 1 - core]
    for u, rows_ref in zip(OFFSETS, rows_refs):
        for i, v in enumerate(OFFSETS):
            dx, dz = jnp.where(core == 0, u, v), jnp.where(core == 0, v, u)
            rows_ref[i] = rows[lax.rem(x + dx + SIDE, SIDE) * SIDE + lax.rem(z + dz + SIDE, SIDE)]


def pack(counts, terms):
    slots, orbitals, basis = terms.shape
    depth = slots * orbitals
    window = jax.ShapeDtypeStruct((depth, WIDE), terms.dtype)
    other_windows = jax.ShapeDtypeStruct((SIDE, depth, WIDE), terms.dtype)
    line_rows = jax.ShapeDtypeStruct((SIDE, depth, basis // PLANE), terms.dtype)
    *mine, theirs, rows_0, rows_1, rows_2, rows_3 = pl.pallas_call(
        pack_kernel,
        out_shape=(window,) * SIDE + (other_windows,) + (line_rows,) * SIDE,
        in_specs=[SMEM, VMEM],
        out_specs=(VMEM,) * (2 * SIDE + 1),
        scratch_shapes=[
            pltpu.VMEM((CORES * SIDE, depth, WIDE), terms.dtype),
            pltpu.VMEM((PLANE, depth, basis // PLANE), terms.dtype),
        ],
        compiler_params=pltpu.CompilerParams(vmem_limit_bytes=12 << 20),
        name="pack",
    )(counts, terms)
    return mine, theirs, (rows_0, rows_1, rows_2, rows_3)


def regroup_kernel(*refs):
    for i, in_ref in enumerate(refs[:SIDE]):
        for j, out_ref in enumerate(refs[SIDE:]):
            out_ref[i] = in_ref[j]


def regroup(blocks):
    return pl.pallas_call(
        regroup_kernel,
        out_shape=tuple(jax.ShapeDtypeStruct(block.shape, block.dtype) for block in blocks),
        in_specs=[VMEM] * SIDE,
        out_specs=(VMEM,) * SIDE,
        compiler_params=pltpu.CompilerParams(vmem_limit_bytes=6 << 20),
        name="regroup",
    )(*blocks)


def along_line(blocks, order):
    got = {0: blocks[0]}
    for offset, block in zip(OFFSETS[1:], blocks[1:]):
        got[-offset if offset < 2 else 2] = along_plane(block, order, offset)
    return [got[offset] for offset in OFFSETS]


def pair_kernel(*refs):
    mine_refs, got_ref, out_refs = refs[:SIDE], refs[SIDE], refs[SIDE + 1 :]
    depth = got_ref.shape[1]
    for dy in range(SIDE):
        out_refs[dy][:depth, :] = mine_refs[dy][...]
        out_refs[dy][depth:, :] = got_ref[dy]


def pair(mine, got):
    window = jax.ShapeDtypeStruct((CORES * got.shape[1], WIDE), got.dtype)
    return pl.pallas_call(
        pair_kernel,
        out_shape=(window,) * SIDE,
        in_specs=[VMEM] * (SIDE + 1),
        out_specs=(VMEM,) * SIDE,
        compiler_params=pltpu.CompilerParams(vmem_limit_bytes=6 << 20),
        name="pair",
    )(*mine, got)


OFFSETS = (0, -1, 1, 2)
OWN = tuple((dcore, 0) for dcore in range(CORES))
OTHERS = tuple((dcore, dy) for dy in range(1, SIDE) for dcore in range(CORES))


def at(sources, v, *us):
    return tuple((u, v, *source) for u in us for source in sources)


def gathered(early, late):
    early_before, early_after = along_plane(early, 0, 1), along_plane(early, 0, -1)
    line = join([early, early_before, early_after])
    left, right = along_plane(line, 1, 1), along_plane(line, 1, -1)
    early_far = along_plane(early_before, 0, 1)
    early_far_sides = along_plane(early_far, 1, 1), along_plane(early_far, 1, -1)
    cut = 2 * early.shape[0]
    back = join([right[cut:], early_far_sides[1]])
    opposite = along_plane(left[:cut], 1, 1), along_plane(back, 1, -1)

    before, after = along_plane(late, 0, 1), along_plane(late, 0, -1)
    near = join([before, after])
    far = along_plane(before, 0, 1)
    near_sides = along_plane(near, 1, 1), along_plane(near, 1, -1)
    own_sides = along_plane(late, 1, 1), along_plane(late, 1, -1)
    far_sides = along_plane(far, 1, 1), along_plane(far, 1, -1)
    own_opposite = along_plane(own_sides[0], 1, 1)
    cut = late.shape[0] // 2
    near_opposite = along_plane(near_sides[0][:cut], 1, 1), along_plane(near_sides[1][cut:], 1, -1)
    far_opposite = along_plane(far_sides[1], 1, -1)

    early_opposite = join(opposite)
    first = join([late, near, far, *own_sides])
    middle = join([*far_sides, own_opposite])
    ends = at(OTHERS, 2, -1, 1)
    early_line = sum((at(OWN, v, 0, -1, 1) for v in (0, -1, 1)), ())
    early_line += at(OWN, 0, 2) + at(OWN, -1, 2) + at(OWN, 1, 2)
    return (
        (early_line, join([line, left, right, early_far, *early_far_sides])),
        (at(OWN, 2, 0, -1, 1, 2), early_opposite),
        (at(OTHERS, 0, 0, -1, 1, 2) + at(OTHERS, -1, 0) + at(OTHERS, 1, 0), first),
        (at(OTHERS, -1, -1, 1), near_sides[0]),
        (at(OTHERS, 1, -1, 1), near_sides[1]),
        (at(OTHERS, -1, 2) + at(OTHERS, 1, 2) + at(OTHERS, 2, 0), middle),
        (ends[: len(ends) // 4], near_opposite[0]),
        (ends[len(ends) // 4 :], near_opposite[1]),
        (at(OTHERS, 2, 2), far_opposite),
    )


def arrange_kernel(layout, *refs):
    in_refs, out_refs = refs[: -len(layout)], refs[-len(layout) :]
    depth = in_refs[0].shape[1]
    for blocks, out_ref in zip(layout, out_refs):
        for i, (u, v, dcore, dy) in enumerate(blocks):
            first, second = (u, v) if dcore == 0 else (v, u)
            chip = OFFSETS.index(second) * SIDE + OFFSETS.index(first)
            source = in_refs[dcore][chip] if dy == 0 else in_refs[CORES + dcore][(dy - 1) * PLANE + chip]
            out_ref[i * depth : (i + 1) * depth, :] = source


def arrange(layout, *rows):
    depth, chip_rows = rows[0].shape[1:]
    size = sum(map(len, layout)) * depth * chip_rows * rows[0].dtype.itemsize
    return pl.pallas_call(
        lambda *refs: arrange_kernel(layout, *refs),
        out_shape=tuple(jax.ShapeDtypeStruct((len(blocks) * depth, chip_rows), rows[0].dtype) for blocks in layout),
        in_specs=[VMEM] * len(rows),
        out_specs=(VMEM,) * len(layout),
        compiler_params=pltpu.CompilerParams(vmem_limit_bytes=2 * size + (1 << 20)),
        cost_estimate=pl.CostEstimate(flops=0, bytes_accessed=2 * size, transcendentals=0),
        name="arrange",
    )(*rows)


def halve_kernel(tile_ref, kept_ref, sent_ref):
    rows = kept_ref.shape[0]
    for core in range(CORES):

        @pl.when(lax.axis_index("core") == core)
        def _():
            kept_ref[...] = tile_ref[core * rows : (core + 1) * rows, :]
            sent_ref[...] = tile_ref[(1 - core) * rows : (2 - core) * rows, :]


def halve(tile):
    half = jax.ShapeDtypeStruct((tile.shape[0] // CORES, tile.shape[1]), tile.dtype)
    return pl.pallas_call(
        halve_kernel,
        out_shape=(half, half),
        in_specs=[VMEM],
        out_specs=(VMEM, VMEM),
        compiler_params=pltpu.CompilerParams(vmem_limit_bytes=8 << 20),
        name="halve",
    )(tile)


def assemble_kernel(kept_ref, got_ref, out_ref):
    rest = out_ref.shape[1] - WIDE
    for core in range(CORES):

        @pl.when(lax.axis_index("core") == core)
        def _():
            first, last = (kept_ref, got_ref) if core == 0 else (got_ref, kept_ref)
            out_ref[:, :WIDE] = first[...]
            out_ref[:, WIDE:] = last[:, :rest]


def assemble(kept, got, columns):
    return pl.pallas_call(
        assemble_kernel,
        out_shape=jax.ShapeDtypeStruct((got.shape[0], columns), got.dtype),
        in_specs=[VMEM, VMEM],
        out_specs=VMEM,
        compiler_params=pltpu.CompilerParams(vmem_limit_bytes=8 << 20),
        name="assemble",
    )(kept, got)


def body(b_tensor, aux_counts):
    basis = b_tensor.shape[0]
    mine, theirs, rows = pack(aux_counts, b_tensor.transpose(1, 2, 0))

    got = swap_cores(theirs)
    windows = pair(mine, got)
    others = join([along_y(windows[-dy % SIDE], -dy % SIDE) for dy in range(1, SIDE)])
    rows = along_line(rows, 0)
    rows = regroup(rows)
    rows = along_line(rows, 1)
    rows = join(rows)
    parts = gathered(windows[0], others)

    left, right = along_y(rows, 1), along_y(rows, -1)
    half = PLANE // 2
    far = along_y(left[:half], 1), along_y(right[half:], -1)
    rest = join([right, *far, left])
    other_rows = swap_cores(rows)
    other_rest = swap_cores(rest)

    def product(weight, block):
        return lax.dot_general(weight, block, (((0,), (0,)), ((), ())), preferred_element_type=jnp.float32)

    weights = arrange([terms for terms, _ in parts[:2]], rows, other_rows)
    weights += arrange([terms for terms, _ in parts[2:]], rows, other_rows, rest, other_rest)
    tile = product(weights[0], parts[0][1])
    for i in (3, 4, 1, 2, 6, 7, 5, 8):
        tile = lax.optimization_barrier(tile + product(weights[i], parts[i][1]))

    kept, sent = halve(tile)
    return assemble(kept, swap_cores(sent), basis // SIDE)


def solution(mesh):
    fine = Mesh(mesh.devices.reshape(SIDE, SIDE, SIDE, CORES), ("y", "x", "z", "core"))
    return jax.shard_map(
        body,
        mesh=fine,
        in_specs=(P(None, "y", ("x", "z", "core")), P()),
        out_specs=P(("x", "z", "core"), "y"),
        check_vma=False,
    )
```

```python
import jax
import jax.numpy as jnp
from jax import lax
from jax.experimental import pallas as pl
from jax.experimental.pallas import tpu as pltpu
from jax.sharding import Mesh, PartitionSpec as P


SIDE = 4
CORES = 2
PLANE = SIDE * SIDE
WIDE = 1280
VMEM = pl.BlockSpec(memory_space=pltpu.VMEM)
SMEM = pl.BlockSpec(memory_space=pltpu.SMEM)


def along_y(block, step):
    return lax.ppermute(block, "y", [(i, (i + step) % SIDE) for i in range(SIDE)])


def swap_cores(block):
    return lax.ppermute(block, "core", [(0, 1), (1, 0)])


def along_plane(block, order, step):
    route = []
    for x in range(SIDE):
        for z in range(SIDE):
            for core in range(CORES):
                to = ((x + step) % SIDE, z) if core == order else (x, (z + step) % SIDE)
                route.append(((x * SIDE + z) * CORES + core, (to[0] * SIDE + to[1]) * CORES + core))
    return lax.ppermute(block, ("x", "z", "core"), route)


def join(blocks):
    def kernel(*refs):
        at = 0
        for ref in refs[:-1]:
            refs[-1][at : at + ref.shape[0]] = ref[...]
            at += ref.shape[0]

    total = sum(block.shape[0] for block in blocks)
    joined = jax.ShapeDtypeStruct((total, *blocks[0].shape[1:]), blocks[0].dtype)
    size = joined.size * joined.dtype.itemsize
    return pl.pallas_call(
        kernel,
        out_shape=joined,
        in_specs=[VMEM] * len(blocks),
        out_specs=VMEM,
        compiler_params=pltpu.CompilerParams(vmem_limit_bytes=2 * size + (1 << 18)),
        cost_estimate=pl.CostEstimate(flops=0, bytes_accessed=2 * size, transcendentals=0),
        name="join",
    )(*blocks)


def pack_kernel(count_ref, terms_ref, *refs):
    mine_refs, theirs_ref, rows_refs, (windows, rows) = refs[:SIDE], refs[SIDE], refs[SIDE + 1 : -2], refs[-2:]
    slots, orbitals, basis = terms_ref.shape
    columns = basis // SIDE
    chip_rows = rows.shape[2]
    x, y, z, core = (lax.axis_index(name) for name in ("x", "y", "z", "core"))
    for s in range(slots):
        live = s < count_ref[y]
        at = pl.ds(s * orbitals, orbitals)
        for p in range(SIDE):
            for q in range(CORES):
                start = p * columns + q * WIDE
                width = min(WIDE, basis - start)
                block = terms_ref[s, :, start : start + width]
                windows[p * CORES + q, at, :width] = jnp.where(live, block, jnp.zeros_like(block))
                if width < WIDE:
                    windows[p * CORES + q, at, width:] = jnp.zeros((orbitals, WIDE - width), block.dtype)
        for i in range(PLANE):
            block = terms_ref[s, :, i * chip_rows : (i + 1) * chip_rows]
            rows[i, at, :] = jnp.where(live, block, jnp.zeros_like(block))
    for dy in range(SIDE):
        plane = lax.rem(y + dy, SIDE) * CORES
        mine_refs[dy][...] = windows[plane + core]
        theirs_ref[dy] = windows[plane + 1 - core]
    for u, rows_ref in zip(OFFSETS, rows_refs):
        for i, v in enumerate(OFFSETS):
            dx, dz = jnp.where(core == 0, u, v), jnp.where(core == 0, v, u)
            rows_ref[i] = rows[lax.rem(x + dx + SIDE, SIDE) * SIDE + lax.rem(z + dz + SIDE, SIDE)]


def pack(counts, terms):
    slots, orbitals, basis = terms.shape
    depth = slots * orbitals
    window = jax.ShapeDtypeStruct((depth, WIDE), terms.dtype)
    other_windows = jax.ShapeDtypeStruct((SIDE, depth, WIDE), terms.dtype)
    line_rows = jax.ShapeDtypeStruct((SIDE, depth, basis // PLANE), terms.dtype)
    *mine, theirs, rows_0, rows_1, rows_2, rows_3 = pl.pallas_call(
        pack_kernel,
        out_shape=(window,) * SIDE + (other_windows,) + (line_rows,) * SIDE,
        in_specs=[SMEM, VMEM],
        out_specs=(VMEM,) * (2 * SIDE + 1),
        scratch_shapes=[
            pltpu.VMEM((CORES * SIDE, depth, WIDE), terms.dtype),
            pltpu.VMEM((PLANE, depth, basis // PLANE), terms.dtype),
        ],
        compiler_params=pltpu.CompilerParams(vmem_limit_bytes=12 << 20),
        name="pack",
    )(counts, terms)
    return mine, theirs, (rows_0, rows_1, rows_2, rows_3)


def regroup_kernel(*refs):
    for i, in_ref in enumerate(refs[:SIDE]):
        for j, out_ref in enumerate(refs[SIDE:]):
            out_ref[i] = in_ref[j]


def regroup(blocks):
    return pl.pallas_call(
        regroup_kernel,
        out_shape=tuple(jax.ShapeDtypeStruct(block.shape, block.dtype) for block in blocks),
        in_specs=[VMEM] * SIDE,
        out_specs=(VMEM,) * SIDE,
        compiler_params=pltpu.CompilerParams(vmem_limit_bytes=6 << 20),
        name="regroup",
    )(*blocks)


def along_line(blocks, order):
    got = {0: blocks[0]}
    for offset, block in zip(OFFSETS[1:], blocks[1:]):
        got[-offset if offset < 2 else 2] = along_plane(block, order, offset)
    return [got[offset] for offset in OFFSETS]


def pair_kernel(*refs):
    mine_refs, got_ref, out_refs = refs[:SIDE], refs[SIDE], refs[SIDE + 1 :]
    depth = got_ref.shape[1]
    for dy in range(SIDE):
        out_refs[dy][:depth, :] = mine_refs[dy][...]
        out_refs[dy][depth:, :] = got_ref[dy]


def pair(mine, got):
    window = jax.ShapeDtypeStruct((CORES * got.shape[1], WIDE), got.dtype)
    return pl.pallas_call(
        pair_kernel,
        out_shape=(window,) * SIDE,
        in_specs=[VMEM] * (SIDE + 1),
        out_specs=(VMEM,) * SIDE,
        compiler_params=pltpu.CompilerParams(vmem_limit_bytes=6 << 20),
        name="pair",
    )(*mine, got)


OFFSETS = (0, -1, 1, 2)
OWN = tuple((dcore, 0) for dcore in range(CORES))
OTHERS = tuple((dcore, dy) for dy in range(1, SIDE) for dcore in range(CORES))


def at(v, *us):
    return tuple((u, v) for u in us)


def gathered_briefly(own):
    before, after, far = (along_plane(own, 0, step) for step in (1, -1, 2))
    line = join([own, before, after, far])
    left, right = along_plane(line, 1, 1), along_plane(line, 1, -1)
    cut = line.shape[0] // 2
    opposite = along_plane(left[:cut], 1, 1), along_plane(right[cut:], 1, -1)
    first = sum((at(v, 0, -1, 1, 2) for v in (0, -1, 1)), ())
    last = join(opposite)
    return (first, join([line, left, right])), (at(2, 0, -1, 1, 2), last)


def gathered(own):
    cut = own.shape[0] // 2
    before, after = along_plane(own, 0, 1), along_plane(own, 0, -1)
    near = join([before, after])
    far = along_plane(before, 0, 1)
    near_sides = along_plane(near, 1, 1), along_plane(near, 1, -1)
    own_sides = along_plane(own, 1, 1), along_plane(own, 1, -1)
    far_sides = along_plane(far, 1, 1), along_plane(far, 1, -1)
    own_opposite = along_plane(own_sides[0], 1, 1)
    near_opposite = along_plane(near_sides[0][:cut], 1, 1), along_plane(near_sides[1][cut:], 1, -1)
    far_opposite = along_plane(far_sides[1], 1, -1)

    first = at(0, 0, -1, 1, 2) + at(-1, 0) + at(1, 0)
    parts = [(first, 0, join([own, near, far, *own_sides]))]
    parts += [(at(v, -1, 1), 0, block) for v, block in zip((-1, 1), near_sides)]
    parts += [(at(-1, 2) + at(1, 2) + at(2, 0), 0, join([*far_sides, own_opposite]))]
    parts += [(at(2, -1, 1), 0, near_opposite[0]), (at(2, -1, 1), len(OTHERS) // 2, near_opposite[1])]
    parts += [(at(2, 2), 0, far_opposite)]
    return parts


def arrange_kernel(layout, *refs):
    in_refs, out_refs = refs[: -len(layout)], refs[-len(layout) :]
    depth = in_refs[0].shape[1]
    for blocks, out_ref in zip(layout, out_refs):
        for i, (u, v, dcore, place) in enumerate(blocks):
            first, second = (u, v) if dcore == 0 else (v, u)
            chip = OFFSETS.index(second) * SIDE + OFFSETS.index(first)
            out_ref[i * depth : (i + 1) * depth, :] = in_refs[dcore][place * PLANE + chip]


def arrange(layout, *rows):
    depth, chip_rows = rows[0].shape[1:]
    size = sum(map(len, layout)) * depth * chip_rows * rows[0].dtype.itemsize
    return pl.pallas_call(
        lambda *refs: arrange_kernel(layout, *refs),
        out_shape=tuple(jax.ShapeDtypeStruct((len(blocks) * depth, chip_rows), rows[0].dtype) for blocks in layout),
        in_specs=[VMEM] * CORES,
        out_specs=(VMEM,) * len(layout),
        compiler_params=pltpu.CompilerParams(vmem_limit_bytes=2 * size + (1 << 20)),
        cost_estimate=pl.CostEstimate(flops=0, bytes_accessed=2 * size, transcendentals=0),
        name="arrange",
    )(*rows)


def halve_kernel(tile_ref, kept_ref, sent_ref):
    rows = kept_ref.shape[0]
    for core in range(CORES):

        @pl.when(lax.axis_index("core") == core)
        def _():
            kept_ref[...] = tile_ref[core * rows : (core + 1) * rows, :]
            sent_ref[...] = tile_ref[(1 - core) * rows : (2 - core) * rows, :]


def halve(tile):
    half = jax.ShapeDtypeStruct((tile.shape[0] // CORES, tile.shape[1]), tile.dtype)
    return pl.pallas_call(
        halve_kernel,
        out_shape=(half, half),
        in_specs=[VMEM],
        out_specs=(VMEM, VMEM),
        compiler_params=pltpu.CompilerParams(vmem_limit_bytes=8 << 20),
        name="halve",
    )(tile)


def write_kernel(half_ref, *refs):
    refs[-1][...] = half_ref[...]


def write(flip, half, columns, out=None):
    args = (half,) if out is None else (half, out)
    rows = half.shape[0]
    return pl.pallas_call(
        write_kernel,
        grid=(1,),
        out_shape=jax.ShapeDtypeStruct((rows, columns), half.dtype),
        in_specs=[pl.BlockSpec((rows, WIDE), lambda i: (0, 0)), pl.BlockSpec(memory_space=pltpu.HBM)][: len(args)],
        out_specs=pl.BlockSpec((rows, WIDE), lambda i: (0, lax.rem(lax.axis_index("core") + flip, CORES))),
        input_output_aliases={} if out is None else {1: 0},
        compiler_params=pltpu.CompilerParams(vmem_limit_bytes=8 << 20),
        cost_estimate=pl.CostEstimate(flops=0, bytes_accessed=2 * half.size * 4, transcendentals=0),
        name="write",
    )(*args)


def body(b_tensor, aux_counts):
    basis = b_tensor.shape[0]
    mine, theirs, rows = pack(aux_counts, b_tensor.transpose(1, 2, 0))

    got = swap_cores(theirs)
    windows = pair(mine, got)
    others = join([along_y(windows[-dy % SIDE], -dy % SIDE) for dy in range(1, SIDE)])
    rows = along_line(rows, 0)
    rows = regroup(rows)
    rows = along_line(rows, 1)
    rows = join(rows)
    early = gathered_briefly(windows[0])
    parts = gathered(others)

    left, right = along_y(rows, 1), along_y(rows, -1)
    half = PLANE // 2
    far = along_y(left[:half], 1), along_y(right[half:], -1)
    rest = join([right, *far, left])
    other_rows = swap_cores(rows)
    other_rest = swap_cores(rest)

    def product(weight, block):
        return lax.dot_general(weight, block, (((0,), (0,)), ((), ())), preferred_element_type=jnp.float32)

    layout = [[(u, v, dcore, dy) for u, v in offsets for dcore, dy in OWN] for offsets, _ in early]
    weights = arrange(layout, rows, other_rows)
    tile = product(weights[0], early[0][1])
    layout = []
    for offsets, skipped, block in parts:
        blocks = [(u, v, dcore, dy - 1) for u, v in offsets for dcore, dy in OTHERS]
        layout.append(blocks[skipped : skipped + block.shape[0] // rows.shape[1]])
    weights = (*arrange(layout, rest, other_rest), weights[1])
    blocks = [block for *_, block in parts] + [early[1][1]]
    for i in (1, 2, len(parts), 0, 4, 5, 3, *range(6, len(parts))):
        tile = lax.optimization_barrier(tile + product(weights[i], blocks[i]))

    kept, sent = halve(tile)
    got = swap_cores(sent)
    out = write(0, kept, basis // SIDE)
    return write(1, got, basis // SIDE, out)


def solution(mesh):
    fine = Mesh(mesh.devices.reshape(SIDE, SIDE, SIDE, CORES), ("y", "x", "z", "core"))
    return jax.shard_map(
        body,
        mesh=fine,
        in_specs=(P(None, "y", ("x", "z", "core")), P()),
        out_specs=P(("x", "z", "core"), "y"),
        check_vma=False,
    )
```

```python
import jax
import jax.numpy as jnp
from jax import lax
from jax.experimental import pallas as pl
from jax.experimental.pallas import tpu as pltpu
from jax.sharding import Mesh, PartitionSpec as P


SIDE = 4
CORES = 2
PLANE = SIDE * SIDE
WIDE = 1280
VMEM = pl.BlockSpec(memory_space=pltpu.VMEM)
SMEM = pl.BlockSpec(memory_space=pltpu.SMEM)


def along_y(block, step):
    return lax.ppermute(block, "y", [(i, (i + step) % SIDE) for i in range(SIDE)])


def swap_cores(block):
    return lax.ppermute(block, "core", [(0, 1), (1, 0)])


def along_plane(block, order, step):
    route = []
    for x in range(SIDE):
        for z in range(SIDE):
            for core in range(CORES):
                to = ((x + step) % SIDE, z) if core == order else (x, (z + step) % SIDE)
                route.append(((x * SIDE + z) * CORES + core, (to[0] * SIDE + to[1]) * CORES + core))
    return lax.ppermute(block, ("x", "z", "core"), route)


def join(blocks):
    def kernel(*refs):
        at = 0
        for ref in refs[:-1]:
            refs[-1][at : at + ref.shape[0]] = ref[...]
            at += ref.shape[0]

    total = sum(block.shape[0] for block in blocks)
    joined = jax.ShapeDtypeStruct((total, *blocks[0].shape[1:]), blocks[0].dtype)
    size = joined.size * joined.dtype.itemsize
    return pl.pallas_call(
        kernel,
        out_shape=joined,
        in_specs=[VMEM] * len(blocks),
        out_specs=VMEM,
        compiler_params=pltpu.CompilerParams(vmem_limit_bytes=2 * size + (1 << 18)),
        cost_estimate=pl.CostEstimate(flops=0, bytes_accessed=2 * size, transcendentals=0),
        name="join",
    )(*blocks)


def pack_kernel(count_ref, terms_ref, *refs):
    mine_refs, theirs_ref, rows_refs, (windows, rows) = refs[:SIDE], refs[SIDE], refs[SIDE + 1 : -2], refs[-2:]
    slots, orbitals, basis = terms_ref.shape
    columns = basis // SIDE
    chip_rows = rows.shape[2]
    x, y, z, core = (lax.axis_index(name) for name in ("x", "y", "z", "core"))
    for s in range(slots):
        live = s < count_ref[y]
        at = pl.ds(s * orbitals, orbitals)
        for p in range(SIDE):
            for q in range(CORES):
                start = p * columns + q * WIDE
                width = min(WIDE, basis - start)
                block = terms_ref[s, :, start : start + width]
                windows[p * CORES + q, at, :width] = jnp.where(live, block, jnp.zeros_like(block))
                if width < WIDE:
                    windows[p * CORES + q, at, width:] = jnp.zeros((orbitals, WIDE - width), block.dtype)
        for i in range(PLANE):
            block = terms_ref[s, :, i * chip_rows : (i + 1) * chip_rows]
            rows[i, at, :] = jnp.where(live, block, jnp.zeros_like(block))
    for dy in range(SIDE):
        plane = lax.rem(y + dy, SIDE) * CORES
        mine_refs[dy][...] = windows[plane + core]
        theirs_ref[dy] = windows[plane + 1 - core]
    for u, rows_ref in zip(OFFSETS, rows_refs):
        for i, v in enumerate(OFFSETS):
            dx, dz = jnp.where(core == 0, u, v), jnp.where(core == 0, v, u)
            rows_ref[i] = rows[lax.rem(x + dx + SIDE, SIDE) * SIDE + lax.rem(z + dz + SIDE, SIDE)]


def pack(counts, terms):
    slots, orbitals, basis = terms.shape
    depth = slots * orbitals
    window = jax.ShapeDtypeStruct((depth, WIDE), terms.dtype)
    other_windows = jax.ShapeDtypeStruct((SIDE, depth, WIDE), terms.dtype)
    line_rows = jax.ShapeDtypeStruct((SIDE, depth, basis // PLANE), terms.dtype)
    *mine, theirs, rows_0, rows_1, rows_2, rows_3 = pl.pallas_call(
        pack_kernel,
        out_shape=(window,) * SIDE + (other_windows,) + (line_rows,) * SIDE,
        in_specs=[SMEM, VMEM],
        out_specs=(VMEM,) * (2 * SIDE + 1),
        scratch_shapes=[
            pltpu.VMEM((CORES * SIDE, depth, WIDE), terms.dtype),
            pltpu.VMEM((PLANE, depth, basis // PLANE), terms.dtype),
        ],
        compiler_params=pltpu.CompilerParams(vmem_limit_bytes=12 << 20),
        name="pack",
    )(counts, terms)
    return mine, theirs, (rows_0, rows_1, rows_2, rows_3)


def regroup_kernel(*refs):
    for i, in_ref in enumerate(refs[:SIDE]):
        for j, out_ref in enumerate(refs[SIDE:]):
            out_ref[i] = in_ref[j]


def regroup(blocks):
    return pl.pallas_call(
        regroup_kernel,
        out_shape=tuple(jax.ShapeDtypeStruct(block.shape, block.dtype) for block in blocks),
        in_specs=[VMEM] * SIDE,
        out_specs=(VMEM,) * SIDE,
        compiler_params=pltpu.CompilerParams(vmem_limit_bytes=6 << 20),
        name="regroup",
    )(*blocks)


def along_line(blocks, order):
    got = {0: blocks[0]}
    for offset, block in zip(OFFSETS[1:], blocks[1:]):
        got[-offset if offset < 2 else 2] = along_plane(block, order, offset)
    return [got[offset] for offset in OFFSETS]


def pair_kernel(*refs):
    mine_refs, got_ref, out_refs = refs[:SIDE], refs[SIDE], refs[SIDE + 1 :]
    depth = got_ref.shape[1]
    for dy in range(SIDE):
        out_refs[dy][:depth, :] = mine_refs[dy][...]
        out_refs[dy][depth:, :] = got_ref[dy]


def pair(mine, got):
    window = jax.ShapeDtypeStruct((CORES * got.shape[1], WIDE), got.dtype)
    return pl.pallas_call(
        pair_kernel,
        out_shape=(window,) * SIDE,
        in_specs=[VMEM] * (SIDE + 1),
        out_specs=(VMEM,) * SIDE,
        compiler_params=pltpu.CompilerParams(vmem_limit_bytes=6 << 20),
        name="pair",
    )(*mine, got)


OFFSETS = (0, -1, 1, 2)
OWN = tuple((dcore, 0) for dcore in range(CORES))
OTHERS = tuple((dcore, dy) for dy in range(1, SIDE) for dcore in range(CORES))


def at(v, *us):
    return tuple((u, v) for u in us)


def gathered_briefly(own):
    before, after, far = (along_plane(own, 0, step) for step in (1, -1, 2))
    line = join([own, before, after, far])
    left, right = along_plane(line, 1, 1), along_plane(line, 1, -1)
    cut = line.shape[0] // 2
    opposite = along_plane(left[:cut], 1, 1), along_plane(right[cut:], 1, -1)
    first = sum((at(v, 0, -1, 1, 2) for v in (0, -1, 1)), ())
    last = join(opposite)
    return (first, join([line, left, right])), (at(2, 0, -1, 1, 2), last)


def gathered(own):
    cut = own.shape[0] // 2
    before, after = along_plane(own, 0, 1), along_plane(own, 0, -1)
    near = join([before, after])
    far = along_plane(before, 0, 1)
    near_sides = along_plane(near, 1, 1), along_plane(near, 1, -1)
    own_sides = along_plane(own, 1, 1), along_plane(own, 1, -1)
    far_sides = along_plane(far, 1, 1), along_plane(far, 1, -1)
    own_opposite = along_plane(own_sides[0], 1, 1)
    near_opposite = along_plane(near_sides[0][:cut], 1, 1), along_plane(near_sides[1][cut:], 1, -1)
    far_opposite = along_plane(far_sides[1], 1, -1)

    first = at(0, 0, -1, 1, 2) + at(-1, 0) + at(1, 0)
    parts = [(first, 0, join([own, near, far, *own_sides]))]
    parts += [(at(v, -1, 1), 0, block) for v, block in zip((-1, 1), near_sides)]
    parts += [(at(-1, 2) + at(1, 2), 0, join(far_sides))]
    parts += [(at(2, -1, 1), 0, near_opposite[0]), (at(2, -1, 1), len(OTHERS) // 2, near_opposite[1])]
    parts += [(at(2, 2), 0, far_opposite), (at(2, 0), 0, own_opposite)]
    return parts


def arrange_kernel(layout, *refs):
    in_refs, out_refs = refs[: -len(layout)], refs[-len(layout) :]
    depth = in_refs[0].shape[1]
    for blocks, out_ref in zip(layout, out_refs):
        for i, (u, v, dcore, place) in enumerate(blocks):
            first, second = (u, v) if dcore == 0 else (v, u)
            chip = OFFSETS.index(second) * SIDE + OFFSETS.index(first)
            out_ref[i * depth : (i + 1) * depth, :] = in_refs[dcore][place * PLANE + chip]


def arrange(layout, *rows):
    depth, chip_rows = rows[0].shape[1:]
    size = sum(map(len, layout)) * depth * chip_rows * rows[0].dtype.itemsize
    return pl.pallas_call(
        lambda *refs: arrange_kernel(layout, *refs),
        out_shape=tuple(jax.ShapeDtypeStruct((len(blocks) * depth, chip_rows), rows[0].dtype) for blocks in layout),
        in_specs=[VMEM] * CORES,
        out_specs=(VMEM,) * len(layout),
        compiler_params=pltpu.CompilerParams(vmem_limit_bytes=2 * size + (1 << 20)),
        cost_estimate=pl.CostEstimate(flops=0, bytes_accessed=2 * size, transcendentals=0),
        name="arrange",
    )(*rows)


def halve_kernel(tile_ref, kept_ref, sent_ref):
    rows = kept_ref.shape[0]
    for core in range(CORES):

        @pl.when(lax.axis_index("core") == core)
        def _():
            kept_ref[...] = tile_ref[core * rows : (core + 1) * rows, :]
            sent_ref[...] = tile_ref[(1 - core) * rows : (2 - core) * rows, :]


def halve(tile):
    half = jax.ShapeDtypeStruct((tile.shape[0] // CORES, tile.shape[1]), tile.dtype)
    return pl.pallas_call(
        halve_kernel,
        out_shape=(half, half),
        in_specs=[VMEM],
        out_specs=(VMEM, VMEM),
        compiler_params=pltpu.CompilerParams(vmem_limit_bytes=8 << 20),
        name="halve",
    )(tile)


def write_kernel(half_ref, *refs):
    refs[-1][...] = half_ref[...]


def write(flip, half, columns, out=None):
    args = (half,) if out is None else (half, out)
    rows = half.shape[0]
    return pl.pallas_call(
        write_kernel,
        grid=(1,),
        out_shape=jax.ShapeDtypeStruct((rows, columns), half.dtype),
        in_specs=[pl.BlockSpec((rows, WIDE), lambda i: (0, 0)), pl.BlockSpec(memory_space=pltpu.HBM)][: len(args)],
        out_specs=pl.BlockSpec((rows, WIDE), lambda i: (0, lax.rem(lax.axis_index("core") + flip, CORES))),
        input_output_aliases={} if out is None else {1: 0},
        compiler_params=pltpu.CompilerParams(vmem_limit_bytes=8 << 20),
        cost_estimate=pl.CostEstimate(flops=0, bytes_accessed=2 * half.size * 4, transcendentals=0),
        name="write",
    )(*args)


def body(b_tensor, aux_counts):
    basis = b_tensor.shape[0]
    mine, theirs, rows = pack(aux_counts, b_tensor.transpose(1, 2, 0))

    got = swap_cores(theirs)
    windows = pair(mine, got)
    others = join([along_y(windows[-dy % SIDE], -dy % SIDE) for dy in range(1, SIDE)])
    rows = along_line(rows, 0)
    rows = regroup(rows)
    rows = along_line(rows, 1)
    rows = join(rows)
    early = gathered_briefly(windows[0])
    parts = gathered(others)

    left, right = along_y(rows, 1), along_y(rows, -1)
    half = PLANE // 2
    far = along_y(left[:half], 1), along_y(right[half:], -1)
    rest = join([right, *far, left])
    other_rows = swap_cores(rows)
    other_rest = swap_cores(rest)

    def product(weight, block):
        return lax.dot_general(weight, block, (((0,), (0,)), ((), ())), preferred_element_type=jnp.float32)

    layout = [[(u, v, dcore, dy) for u, v in offsets for dcore, dy in OWN] for offsets, _ in early]
    weights = arrange(layout, rows, other_rows)
    tile = product(weights[0], early[0][1])
    layout = []
    for offsets, skipped, block in parts:
        blocks = [(u, v, dcore, dy - 1) for u, v in offsets for dcore, dy in OTHERS]
        layout.append(blocks[skipped : skipped + block.shape[0] // rows.shape[1]])
    weights = (*arrange(layout, rest, other_rest), weights[1])
    blocks = [block for *_, block in parts] + [early[1][1]]
    for i in (1, 2, len(parts), 3, 0, *range(4, len(parts))):
        tile = lax.optimization_barrier(tile + product(weights[i], blocks[i]))

    kept, sent = halve(tile)
    got = swap_cores(sent)
    out = write(0, kept, basis // SIDE)
    return write(1, got, basis // SIDE, out)


def solution(mesh):
    fine = Mesh(mesh.devices.reshape(SIDE, SIDE, SIDE, CORES), ("y", "x", "z", "core"))
    return jax.shard_map(
        body,
        mesh=fine,
        in_specs=(P(None, "y", ("x", "z", "core")), P()),
        out_specs=P(("x", "z", "core"), "y"),
        check_vma=False,
    )
```
